32 devices in a mesh: group: 2 (over y), role: 2 (over core), dev: 8 (over z, x).
Axes of the slice: x: 2, y: 2, z: 4, core: 2. Of those that a mesh axis runs over, the one named last changes fastest.
Arguments:
- hidden: bfloat16 [64, 7168], P(('group', 'role', 'dev')), parts along dimension 0, may hold values from -6 to 6
- norm_gain: bfloat16 [7168], replicated, may hold values from 0.099609375 to 1.8984375
- routes: int32 [64, 8], P(('group', 'role', 'dev')), parts along dimension 0, may hold values from 0 to 15, all different within a row; in each aligned block of 2 rows (0 to 1, 2 to 3, ...) at most 2 rows name the same one
- gate_weights: float32 [64, 8], P(('group', 'role', 'dev')), parts along dimension 0, may hold values from 0.1 to 0.5
- w_gate: bfloat16 [7168, 32768], P(None, ('role', 'dev')), may hold values from -0.0625 to 0.0625
- w_up: bfloat16 [7168, 32768], P(None, ('role', 'dev')), may hold values from -0.0625 to 0.0625
- w_down: bfloat16 [32768, 7168], P(('role', 'dev')), may hold values from -0.125 to 0.125
- queries: bfloat16 [64, 64, 576], P(('group', 'role', 'dev')), parts along dimension 0, may hold values from -48 to 48
- local_cache: bfloat16 [64, 64, 576], P(('group', 'role', 'dev')), parts along dimension 0, may hold values from -6 to 6
- cache_lengths: int32 [64], P(('group', 'role', 'dev')), parts along dimension 0, may hold values from 2 to 64
- swap_pool: bfloat16 [512, 16, 576], P(('group', 'role', 'dev')), parts along dimension 0, may hold values from -6 to 6
- page_ids: int32 [32, 16], P(('group', 'role', 'dev')), parts along dimension 0, may hold values from 0 to 15
- page_owner: int32 [32, 16], P(('group', 'role', 'dev')), parts along dimension 0, may hold values from 0 to 1
Outputs:
- attn_out: bfloat16 [64, 64, 512], P(('group', 'role', 'dev')), parts along dimension 0
- moe_out: bfloat16 [64, 7168], P(('group', 'role', 'dev')), parts along dimension 0
The draws below stay inside these ranges and needn't reach their ends.
There are 2 independent parts, one for each index of `group`. The reference program is written for one: setup_inputs(seed, part) draws one part's arguments, and reference() takes and returns one part's arrays. A program takes and returns all parts, laid end to end along the dimension named above; an argument that names none is the same for every part. Nothing has to cross between parts.
Inputs may be any that keep to these rules, and one draw needn't show every extreme that they name: `routes`: each row names 8 different experts; in the rows of one device no expert is named more than 2 times. `page_ids`: every device receives exactly one page from every holder.
All inputs are finite; a program needn't handle non-finite values.
Results may differ from the reference program's by a relative error of at most 0.0046.
Values may be sent and summed in bfloat16 or wider, within the bound.
No kernel may reach another device: no remote copies, remote signals or barrier semaphores. Data moves between devices by JAX's collectives and lax.ppermute only.
A program may use at most 128 MiB of HBM per device.

```python
import math
import jax
import jax.numpy as jnp
import numpy as np
from jax import lax

D = 7168
LAT = 512
ROPE = 64
EWIN = 2048
TOP = 8
HEADS = 64
EXPERTS = 16
PAGE = 16
REQ_DEV = 2
LOCAL_LEN = 64
POOL = 16
CAP = 2
ROWS = 32
POOL_ALL = 256
N_ROLE = 2
N_DEV = 8


def attention_draws(key):
    channels = LAT + ROPE
    subkeys = jax.random.split(jax.random.fold_in(key, 9151), 2)
    latents = jnp.clip(jax.random.normal(subkeys[0], (ROWS, LOCAL_LEN, channels), jnp.float32), -6.0, 6.0)
    queries = jnp.clip(jax.random.normal(subkeys[1], (ROWS, HEADS, channels), jnp.float32), -6.0, 6.0)
    return (queries, latents)


def draw_queries(key, part):
    return attention_draws(key)[0].astype(jnp.bfloat16)


def draw_local_cache(key, part):
    return attention_draws(key)[1].astype(jnp.bfloat16)


def plant(array, rng, low, largest):
    spot = [jax.random.randint(jax.random.fold_in(rng, axis), (), 0, length) for axis, length in enumerate(array.shape)]
    main_axis = array.shape.index(max(array.shape))
    neighbour = spot[:main_axis] + [(spot[main_axis] + 1) % array.shape[main_axis]] + spot[main_axis + 1:]
    return array.at[tuple(spot)].set(low).at[tuple(neighbour)].set(largest)


def levels(own_key, extent, pieces, smallest, top_value):
    gain, own = 1.0, jax.random.fold_in(own_key, 6)
    for dim, blocks in pieces:
        heights = jnp.exp(jax.random.uniform(jax.random.fold_in(own, dim), (blocks,), jnp.float32, smallest / len(pieces), top_value / len(pieces)))
        gain = gain * jnp.repeat(heights, extent[dim] // blocks).reshape([-1 if axis == dim else 1 for axis in range(len(extent))])
    return gain


def cumulative_ranks(number_of, slope):
    portions = [(1 << 20) // math.isqrt(standing ** slope) + 1 for standing in range(1, number_of + 1)]
    width = 1 + sum(portions) // (1 << 30)
    return np.cumsum(np.array([max(1, weight // width) for weight in portions]))


def skewed_ids(rng, dims, amount, slope):
    table = cumulative_ranks(amount, slope)
    ticket = jax.random.randint(jax.random.fold_in(rng, 1), dims, 0, int(table[amount - 1]))
    grade = jnp.searchsorted(jnp.asarray(table, jnp.int32), ticket, side="right")
    return jax.random.permutation(jax.random.fold_in(rng, 2), amount)[grade].astype(jnp.int32)


def routed_block(own_key, own, number, rows, number_of, top, most, slope):
    ranking = jax.random.permutation(own_key, number_of)
    heavy_load, ordinary = portions_of(number_of, rows * top, most, slope, True), portions_of(number_of, rows * top, most, slope, False)
    places = jnp.arange(number_of)

    def named(sizes, offset_by):
        used = int((sizes > 0).sum())
        fixed = max(1, used // 4)
        moved = fixed + (places - fixed + offset_by * (used - fixed)) % max(1, number_of - fixed)
        return jnp.zeros((number_of,), jnp.int32).at[ranking[jnp.where(places < fixed, places, moved)]].set(jnp.asarray(sizes, jnp.int32))

    sizes = jnp.where(number % 4 == 0, named(heavy_load, number // 4), named(ordinary, number - number // 4 - 1))
    mixed = jax.random.permutation(jax.random.fold_in(own, 3), number_of)
    giver, sink = mixed[0:number_of // 2 * 2:2], mixed[1:number_of // 2 * 2:2]
    margin = jnp.minimum(sizes[giver] - 1, most - sizes[sink]) // 2
    margin = jnp.where((giver == ranking[0]) | (sink == ranking[0]) | (sizes[sink] == 0), 0, jnp.maximum(margin, 0))
    moved = jax.random.randint(jax.random.fold_in(own, 4), (number_of // 2,), 0, 1 << 20) % (margin + 1)
    sizes = sizes.at[giver].add(-moved).at[sink].add(moved)
    items = jnp.searchsorted(jnp.cumsum(sizes), jnp.arange(rows * top), side="right").astype(jnp.int32)
    table = items.reshape(top, rows).T
    table = table[jax.random.permutation(jax.random.fold_in(own, 1), rows)]
    offset_by = jax.random.randint(jax.random.fold_in(own, 2), (rows, 1), 0, top)
    return jnp.take_along_axis(table, (jnp.arange(top)[None, :] + offset_by) % top, axis=1)


def portions_of(amount, total, most, lean, full):
    loads = [(1 << 20) // math.isqrt(standing ** lean) + 1 for standing in range(1, amount + 1)]
    largest = most if full else min(most, max(-(-total // amount), total * loads[0] // sum(loads)))
    least = 1 if total - largest >= amount - 1 else 0
    given, surplus = [largest] + [least] * (amount - 1), total - largest - least * (amount - 1)
    while surplus > 0:
        movable = [i for i in range(1, amount) if given[i] < largest] or [i for i in range(1, amount) if given[i] < most]
        pool, budget = sum([loads[i] for i in movable]), surplus
        for i in movable:
            more = min(most - given[i], max(1, budget * loads[i] // pool), surplus)
            given[i] = given[i] + more
            surplus = surplus - more
    return np.array(given)


def bell_draw(stream_key, shape, scale, limit, shards=(), kind=jnp.bfloat16):
    values = scale * jax.random.normal(stream_key, shape, jnp.float32)
    if shards:
        values = values * levels(stream_key, shape, shards, -0.22, 0.18)
    return jnp.clip(values, -limit, limit).astype(kind)


def setup_inputs(seed: int = 0, part: int = 0) -> dict:
    streams_of = jax.random.split(jax.random.key(seed), 14)
    part_keys = jax.random.split(jax.random.fold_in(streams_of[13], part), 14)
    hidden = bell_draw(part_keys[0], (ROWS, D), 1.0, 6.0, ((0, 16),))
    norm_gain = jnp.clip(1.0 + 0.18 * jax.random.normal(streams_of[1], (D,), jnp.float32), 0.099609375, 1.8984375).astype(jnp.bfloat16)
    routes_keys = jax.random.split(jax.random.fold_in(part_keys[2], 1), ROWS // REQ_DEV)
    routes_turns = jax.random.permutation(jax.random.fold_in(part_keys[2], 3), ROWS // REQ_DEV)
    routes = jax.vmap(lambda own, number: routed_block(jax.random.fold_in(part_keys[2], 2), own, number, REQ_DEV, EXPERTS, TOP, CAP, 2))(routes_keys, routes_turns).reshape((ROWS, TOP))
    gate_weights = jnp.clip(0.1 + 0.4 * jax.random.uniform(part_keys[3], (ROWS, TOP), jnp.float32) ** levels(part_keys[3], (ROWS, TOP), ((0, 16),), -0.2, 0.2), 0.1, 0.5)
    w_gate = bell_draw(streams_of[4], (D, EXPERTS * EWIN), D ** -0.5, 0.0625, ((1, 16),))
    w_up = bell_draw(streams_of[5], (D, EXPERTS * EWIN), D ** -0.5, 0.0625, ((1, 16),))
    w_down = bell_draw(streams_of[6], (EXPERTS * EWIN, D), EWIN ** -0.5, 0.125, ((0, 16),))
    queries = draw_queries(jax.random.fold_in(jax.random.fold_in(streams_of[13], part), 71), part)
    local_cache = draw_local_cache(jax.random.fold_in(jax.random.fold_in(streams_of[13], part), 71), part)
    cache_lengths = plant(jax.random.randint(part_keys[9], (ROWS,), 2, LOCAL_LEN + 1), jax.random.fold_in(part_keys[9], 1), 2, LOCAL_LEN).astype(jnp.int32)
    swap_pool = bell_draw(part_keys[10], (POOL_ALL, PAGE, LAT + ROPE), 1.0, 6.0, ((0, 16),))
    page_ids = plant(jax.random.randint(part_keys[11], (N_ROLE * N_DEV, N_ROLE * N_DEV), 0, POOL), jax.random.fold_in(part_keys[11], 1), 0, POOL - 1).astype(jnp.int32)
    page_owner = plant(skewed_ids(part_keys[12], (N_ROLE * N_DEV, N_ROLE * N_DEV), REQ_DEV, 2), jax.random.fold_in(part_keys[12], 3), 0, REQ_DEV - 1).astype(jnp.int32)
    return dict(hidden=hidden, norm_gain=norm_gain, routes=routes, gate_weights=gate_weights, w_gate=w_gate, w_up=w_up, w_down=w_down, queries=queries, local_cache=local_cache, cache_lengths=cache_lengths, swap_pool=swap_pool, page_ids=page_ids, page_owner=page_owner)


score_scale = 192.0 ** (-0.5)
norm_eps = 1e-06

def device_attention(queries, local_cache, cache_lengths, fetched, owners):
    query_wide = queries.astype(jnp.float32)
    local_scores = jnp.einsum('rhc,rtc->rht', query_wide, local_cache.astype(jnp.float32)) * score_scale
    positions = jnp.arange(local_cache.shape[1], dtype=jnp.int32)
    local_valid = positions[None, None, :] < cache_lengths[:, None, None]
    local_scores = jnp.where(local_valid, local_scores, -jnp.inf)
    page_query = queries[owners]
    page_scores = jnp.einsum('phc,ptc->pht', page_query.astype(jnp.float32), fetched.astype(jnp.float32)) * score_scale
    request_ids = jnp.arange(queries.shape[0], dtype=jnp.int32)
    belongs = owners[None, :] == request_ids[:, None]
    page_peak = lax.optimization_barrier(jnp.max(page_scores, axis=2))
    owned_peak = lax.optimization_barrier(jnp.max(jnp.where(belongs[:, :, None], page_peak[None], -jnp.inf), axis=1))
    row_peak = jnp.maximum(lax.optimization_barrier(jnp.max(local_scores, axis=2)), owned_peak)
    local_exp = jnp.exp(local_scores - row_peak[:, :, None])
    page_exp = jnp.exp(page_scores - row_peak[owners][:, :, None])
    page_total = lax.optimization_barrier(jnp.sum(page_exp, axis=2))
    owned_total = lax.optimization_barrier(jnp.sum(jnp.where(belongs[:, :, None], page_total[None], 0.0), axis=1))
    normalizer = lax.optimization_barrier(jnp.sum(local_exp, axis=2)) + owned_total
    local_probs = (local_exp / normalizer[:, :, None]).astype(jnp.bfloat16)
    page_probs = (page_exp / normalizer[owners][:, :, None]).astype(jnp.bfloat16)
    local_part = jnp.einsum('rht,rtc->rhc', local_probs.astype(jnp.float32), local_cache[:, :, :LAT].astype(jnp.float32))
    page_part = jnp.einsum('pht,ptc->phc', page_probs.astype(jnp.float32), fetched[:, :, :LAT].astype(jnp.float32))
    owned_part = jnp.einsum('rp,phc->rhc', belongs.astype(jnp.float32), page_part, precision=lax.Precision.HIGHEST)
    return (local_part + owned_part).astype(jnp.bfloat16)

def reference(hidden, norm_gain, routes, gate_weights, w_gate, w_up, w_down, queries, local_cache, cache_lengths, swap_pool, page_ids, page_owner):
    devices = N_ROLE * N_DEV
    channels = LAT + ROPE
    pool_blocks = swap_pool.reshape(devices, POOL, PAGE, channels)
    query_blocks = queries.reshape(devices, REQ_DEV, HEADS, channels)
    cache_blocks = local_cache.reshape(devices, REQ_DEV, LOCAL_LEN, channels)
    length_blocks = cache_lengths.reshape(devices, REQ_DEV)
    sources = jnp.arange(devices, dtype=jnp.int32)

    def one_device(packed):
        query_block, cache_block, length_block, id_row, owner_row = packed
        fetched = pool_blocks[sources, id_row]
        return device_attention(query_block, cache_block, length_block, fetched, owner_row)
    attention = lax.map(one_device, (query_blocks, cache_blocks, length_blocks, page_ids, page_owner))
    attn_out = attention.reshape(ROWS, HEADS, LAT)
    hidden_wide = hidden.astype(jnp.float32)
    inv_rms = lax.rsqrt(lax.optimization_barrier(jnp.mean(hidden_wide * hidden_wide, axis=1, keepdims=True)) + norm_eps)
    normed = (hidden_wide * inv_rms * norm_gain.astype(jnp.float32)[None, :]).astype(jnp.bfloat16)
    expert_ids = jnp.arange(EXPERTS, dtype=jnp.int32)

    def add_expert(running, expert):
        start = (expert * EWIN).astype(jnp.int32)
        gate_cols = lax.dynamic_slice_in_dim(w_gate, start, EWIN, 1)
        up_cols = lax.dynamic_slice_in_dim(w_up, start, EWIN, 1)
        down_rows = lax.dynamic_slice_in_dim(w_down, start, EWIN, 0)
        gate_proj = jnp.dot(normed, gate_cols, preferred_element_type=jnp.float32)
        up_proj = jnp.dot(normed, up_cols, preferred_element_type=jnp.float32)
        act_units = (jax.nn.silu(gate_proj) * up_proj).astype(jnp.bfloat16)
        output = jnp.dot(act_units, down_rows, preferred_element_type=jnp.float32)
        weight = lax.optimization_barrier(jnp.sum(jnp.where(routes == expert, gate_weights, 0.0), axis=1))
        return (running + weight[:, None] * output, None)
    running, _ = lax.scan(add_expert, jnp.zeros((ROWS, D), jnp.float32), expert_ids)
    moe_out = (hidden_wide + running).astype(jnp.bfloat16)
    return (attn_out, moe_out)
```

```python
import functools

import jax
import jax.numpy as jnp
from jax import lax
from jax.experimental import pallas as pl
from jax.experimental.pallas import tpu as pltpu
from jax.sharding import PartitionSpec as P

ROPE = 64
EXPERTS = 16
LANES = 128

score_scale = 192.0 ** (-0.5)
norm_eps = 1e-06


VM = pl.BlockSpec(memory_space=pltpu.VMEM)
SM = pl.BlockSpec(memory_space=pltpu.SMEM)
ANY = pl.BlockSpec(memory_space=pl.ANY)


def exchange_rounds(role_size, dev_size):
    rounds = []
    bit = dev_size // 2
    while bit:
        rounds.append(("dev", bit, dev_size))
        bit //= 2
    bit = role_size // 2
    while bit:
        rounds.append(("role", bit, role_size))
        bit //= 2
    return rounds


def swap(x, rnd):
    axis, bit, size = rnd
    return lax.ppermute(x, axis, [(i, i ^ bit) for i in range(size)])


def pack_kernel(hid_ref, gain_ref, routes_ref, weights_ref, ids_ref, out_ref):
    width = hid_ref.shape[1]
    rows = hid_ref.shape[0]
    extra = out_ref.shape[1] - width
    x = hid_ref[...].astype(jnp.float32)
    inv = lax.rsqrt(jnp.mean(x * x, axis=1, keepdims=True) + norm_eps)
    out_ref[:, :width] = (x * inv * gain_ref[...].astype(jnp.float32)).astype(jnp.bfloat16)
    lane = lax.broadcasted_iota(jnp.int32, (rows, LANES), 1)
    expert = lax.rem(lane, EXPERTS)
    routes = routes_ref[...]
    weights = weights_ref[...]
    weight = jnp.zeros((rows, LANES), jnp.float32)
    for k in range(routes.shape[1]):
        weight = weight + jnp.where(routes[:, k : k + 1] == expert, weights[:, k : k + 1], 0.0)
    high = weight.astype(jnp.bfloat16).astype(jnp.float32)
    tail = jnp.where(lane < EXPERTS, high, jnp.where(lane < 2 * EXPERTS, weight - high, 0.0))
    out_ref[:, width : width + LANES] = tail.astype(jnp.bfloat16)
    ids = ids_ref[...].astype(jnp.float32)
    out_ref[:, width + LANES :] = jnp.broadcast_to(ids, (rows, extra - LANES)).astype(jnp.bfloat16)


def pick_kernel(me_ref, ids_ref, pool_ref, out_ref, sems, *, rounds, role_size, dev_size):
    me = me_ref[0]
    count = out_ref.shape[0]

    def copy(d):
        away = d ^ me
        slot = jnp.int32(0)
        for i, (axis, bit, _) in enumerate(rounds):
            flat = bit if axis == "dev" else bit * dev_size
            slot = slot + jnp.where((away & flat) != 0, jnp.int32(1 << i), jnp.int32(0))
        page = ids_ref[slot, me]
        return pltpu.make_async_copy(pool_ref.at[page], out_ref.at[d], sems.at[d])

    def start(d, c):
        copy(d).start()
        return c

    def wait(d, c):
        pltpu.make_async_copy(pool_ref.at[0], out_ref.at[d], sems.at[d]).wait()
        return c

    lax.fori_loop(0, count, start, 0)
    lax.fori_loop(0, count, wait, 0)


def expert_kernel(
    expert_ref, xa_ref, xb_ref, g_ref, u_ref, d_ref, keep_ref, send_ref,
    gb, ub, db, ga, ua, h, wsel, sem, semd, *, tk, tn, nb, nd,
):
    k_size, f_size = g_ref.shape
    n1, n2 = k_size // tk, k_size // tn
    half = xa_ref.shape[0]

    def cg(i):
        s = lax.rem(i, nb)
        return pltpu.make_async_copy(g_ref.at[pl.ds(i * tk, tk)], gb.at[s], sem.at[0, s])

    def cu(i):
        s = lax.rem(i, nb)
        return pltpu.make_async_copy(u_ref.at[pl.ds(i * tk, tk)], ub.at[s], sem.at[1, s])

    def cd(j):
        s = lax.rem(j, nd)
        cols = pl.ds(pl.multiple_of(j * tn, tn), tn)
        return pltpu.make_async_copy(d_ref.at[:, cols], db.at[s], semd.at[s])

    for i in range(nb):
        cg(i).start()
        cu(i).start()
    ga[...] = jnp.zeros_like(ga)
    ua[...] = jnp.zeros_like(ua)
    lane = lax.broadcasted_iota(jnp.int32, (half, LANES), 1)
    chosen = (lane == expert_ref[0]) | (lane == expert_ref[0] + EXPERTS)
    for i, ref in enumerate((xa_ref, xb_ref)):
        tail = ref[:, k_size : k_size + LANES].astype(jnp.float32)
        wsel[i * half : (i + 1) * half] = jnp.sum(jnp.where(chosen, tail, 0.0), axis=1, keepdims=True)

    def first(i, c):
        s = lax.rem(i, nb)
        cg(i).wait()
        cu(i).wait()
        cols = pl.ds(pl.multiple_of(i * tk, tk), tk)
        xs = jnp.concatenate([xa_ref[:, cols], xb_ref[:, cols]], axis=0)
        ga[...] += jnp.dot(xs, gb[s], preferred_element_type=jnp.float32)
        ua[...] += jnp.dot(xs, ub[s], preferred_element_type=jnp.float32)

        @pl.when(i + nb < n1)
        def _():
            cg(i + nb).start()
            cu(i + nb).start()

        @pl.when(i + nd >= n1)
        def _():
            cd(i + nd - n1).start()

        return c

    lax.fori_loop(0, n1, first, 0)
    g = ga[...]
    h[...] = ((g / (1.0 + jnp.exp(-g))) * ua[...]).astype(jnp.bfloat16)

    def second(j, c):
        s = lax.rem(j, nd)
        cd(j).wait()
        cols = pl.ds(pl.multiple_of(j * tn, tn), tn)
        out = jnp.dot(h[...], db[s], preferred_element_type=jnp.float32)
        out = out * wsel[...]
        keep_ref[:, cols] = out[:half]
        send_ref[:, cols] = out[half:].astype(jnp.bfloat16)

        @pl.when(j + nd < n2)
        def _():
            cd(j + nd).start()

        return c

    lax.fori_loop(0, n2, second, 0)


def attention_kernel(len_ref, owner_ref, q_ref, local_ref, page_ref, out_ref):
    requests, heads, width = q_ref.shape
    value = out_ref.shape[2]
    local_len = local_ref.shape[1]
    pages, page_len, _ = page_ref.shape
    paged = page_ref[...].reshape(pages * page_len, width)
    row = lax.broadcasted_iota(jnp.int32, (pages, pages * page_len), 0)
    col = lax.broadcasted_iota(jnp.int32, (pages, pages * page_len), 1)
    inside = (col >= row * page_len) & (col < (row + 1) * page_len)
    owner = jnp.broadcast_to(jnp.transpose(owner_ref[...].astype(jnp.float32)), inside.shape)
    key_owner = jnp.sum(jnp.where(inside, owner, 0.0), axis=0, keepdims=True)
    nt = (((1,), (1,)), ((), ()))
    for r in range(requests):
        q = q_ref[r]
        local = local_ref[r]
        s_local = lax.dot_general(q, local, nt, preferred_element_type=jnp.float32) * score_scale
        pos = lax.broadcasted_iota(jnp.int32, (heads, local_len), 1)
        s_local = jnp.where(pos < len_ref[r], s_local, -jnp.inf)
        s_page = lax.dot_general(q, paged, nt, preferred_element_type=jnp.float32) * score_scale
        s_page = jnp.where(key_owner == float(r), s_page, -jnp.inf)
        peak = jnp.maximum(jnp.max(s_local, axis=1, keepdims=True), jnp.max(s_page, axis=1, keepdims=True))
        e_local = jnp.exp(s_local - peak)
        e_page = jnp.exp(s_page - peak)
        total = jnp.sum(e_local, axis=1, keepdims=True) + jnp.sum(e_page, axis=1, keepdims=True)
        p_local = (e_local / total).astype(jnp.bfloat16)
        p_page = (e_page / total).astype(jnp.bfloat16)
        out = jnp.dot(p_local, local[:, :value], preferred_element_type=jnp.float32)
        out = out + jnp.dot(p_page, paged[:, :value], preferred_element_type=jnp.float32)
        out_ref[r] = out.astype(jnp.bfloat16)


def tile_of(size, want):
    tile = min(size, want)
    while size % tile:
        tile -= LANES
    return tile


def per_device(
    hidden, norm_gain, routes, gate_weights, w_gate, w_up, w_down,
    queries, local_cache, cache_lengths, swap_pool, page_ids, page_owner,
):
    role_size, dev_size = lax.axis_size("role"), lax.axis_size("dev")
    devices = role_size * dev_size
    slices = devices // EXPERTS
    rounds = exchange_rounds(role_size, dev_size)
    me = lax.axis_index("role") * dev_size + lax.axis_index("dev")
    me_arr = jnp.reshape(me, (1,)).astype(jnp.int32)
    expert_arr = jnp.reshape(me // slices, (1,)).astype(jnp.int32)
    rows, width = hidden.shape
    units = w_gate.shape[1]
    id_cols = pl.cdiv(devices, LANES) * LANES
    packed_width = width + LANES + id_cols
    ids_padded = jnp.pad(page_ids, ((0, 0), (0, id_cols - devices)))
    packed = pl.pallas_call(
        pack_kernel,
        out_shape=jax.ShapeDtypeStruct((rows, packed_width), jnp.bfloat16),
        in_specs=[VM] * 5,
        out_specs=VM,
        compiler_params=pltpu.CompilerParams(vmem_limit_bytes=4 << 20),
    )(hidden, norm_gain.reshape(1, width), routes, gate_weights, ids_padded)

    held = packed[None]
    for rnd in rounds[:-1]:
        held = jnp.concatenate([held, swap(held, rnd)], axis=0)
    held = held.reshape(-1, packed_width)
    other = swap(held, rounds[-1])
    half = held.shape[0]

    ids = jnp.concatenate(
        [held[::rows, width + LANES : width + LANES + devices], other[::rows, width + LANES : width + LANES + devices]],
        axis=0,
    ).astype(jnp.int32)
    outgoing = pl.pallas_call(
        functools.partial(pick_kernel, rounds=rounds, role_size=role_size, dev_size=dev_size),
        out_shape=jax.ShapeDtypeStruct((devices,) + swap_pool.shape[1:], jnp.bfloat16),
        in_specs=[SM, SM, ANY],
        out_specs=VM,
        scratch_shapes=[pltpu.SemaphoreType.DMA((devices,))],
        compiler_params=pltpu.CompilerParams(vmem_limit_bytes=12 << 20),
    )(me_arr, ids, swap_pool)
    arrived = lax.all_to_all(outgoing, ("role", "dev"), split_axis=0, concat_axis=0, tiled=True)

    tk, tn = tile_of(width, 512), tile_of(width, 512)
    nb = nd = 4
    keep, send = pl.pallas_call(
        functools.partial(expert_kernel, tk=tk, tn=tn, nb=nb, nd=nd),
        out_shape=(
            jax.ShapeDtypeStruct((half, width), jnp.float32),
            jax.ShapeDtypeStruct((half, width), jnp.bfloat16),
        ),
        in_specs=[SM, VM, VM, ANY, ANY, ANY],
        out_specs=(VM, VM),
        scratch_shapes=[
            pltpu.VMEM((nb, tk, units), jnp.bfloat16),
            pltpu.VMEM((nb, tk, units), jnp.bfloat16),
            pltpu.VMEM((nd, units, tn), jnp.bfloat16),
            pltpu.VMEM((2 * half, units), jnp.float32),
            pltpu.VMEM((2 * half, units), jnp.float32),
            pltpu.VMEM((2 * half, units), jnp.bfloat16),
            pltpu.VMEM((2 * half, 1), jnp.float32),
            pltpu.SemaphoreType.DMA((2, nb)),
            pltpu.SemaphoreType.DMA((nd,)),
        ],
        compiler_params=pltpu.CompilerParams(vmem_limit_bytes=56 << 20),
        cost_estimate=pl.CostEstimate(
            flops=6 * 2 * half * width * units, bytes_accessed=6 * width * units, transcendentals=0
        ),
    )(expert_arr, held, other, w_gate, w_up, w_down)

    attn_out = pl.pallas_call(
        attention_kernel,
        out_shape=jax.ShapeDtypeStruct(queries.shape[:2] + (queries.shape[2] - ROPE,), jnp.bfloat16),
        in_specs=[SM, VM, VM, VM, VM],
        out_specs=VM,
        compiler_params=pltpu.CompilerParams(vmem_limit_bytes=24 << 20),
        cost_estimate=pl.CostEstimate(flops=1 << 27, bytes_accessed=1 << 20, transcendentals=1 << 16),
    )(cache_lengths, page_owner, queries, local_cache, arrived)

    total = keep + swap(send, rounds[-1]).astype(jnp.float32)
    for rnd in rounds[-2::-1]:
        total = total.reshape(2, -1, rows, width)
        got = swap(total[1].astype(jnp.bfloat16), rnd)
        total = total[0] + got.astype(jnp.float32)
    moe_out = (hidden.astype(jnp.float32) + total.reshape(rows, width)).astype(jnp.bfloat16)
    return (attn_out, moe_out)


def solution(mesh):
    in_specs = (
        P(("group", "role", "dev"), None),
        P(),
        P(("group", "role", "dev"), None),
        P(("group", "role", "dev"), None),
        P(None, ("role", "dev")),
        P(None, ("role", "dev")),
        P(("role", "dev"), None),
        P(("group", "role", "dev"), None, None),
        P(("group", "role", "dev"), None, None),
        P(("group", "role", "dev")),
        P(("group", "role", "dev"), None, None),
        P(("group", "role", "dev"), None),
        P(("group", "role", "dev"), None),
    )
    out_specs = (P(("group", "role", "dev"), None, None), P(("group", "role", "dev"), None))
    return jax.shard_map(
        per_device, mesh=mesh, in_specs=in_specs, out_specs=out_specs, check_vma=False
    )
```

```python
import functools

import jax
import jax.numpy as jnp
from jax import lax
from jax.experimental import pallas as pl
from jax.experimental.pallas import tpu as pltpu
from jax.sharding import PartitionSpec as P


ROPE = 64
EXPERTS = 16
LANES = 128

LOADS = (3,3,3,1)
GATE_SLOTS = 3
UP_SLOTS = 6
DOWN_SLOTS = 6

score_scale = 192.0 ** (-0.5)
norm_eps = 1e-06


VM = pl.BlockSpec(memory_space=pltpu.VMEM)
SM = pl.BlockSpec(memory_space=pltpu.SMEM)
HBM = pl.BlockSpec(memory_space=pltpu.HBM)


def role_swap(x):
    size = lax.axis_size("role")
    return lax.ppermute(x, "role", [(i, size - 1 - i) for i in range(size)])


def pack_kernel(me_ref, hid_ref, gain_ref, routes_ref, weights_ref, ids_ref, out_ref, hid, gain, routes_v, weights_v, ids_v, sems):
    rows, width = hid.shape
    copies = [
        pltpu.make_async_copy(src, dst, sems.at[i])
        for i, (src, dst) in enumerate(
            ((hid_ref, hid), (gain_ref, gain), (routes_ref, routes_v), (weights_ref, weights_v), (ids_ref, ids_v))
        )
    ]
    for c in copies:
        c.start()
    for c in copies:
        c.wait()
    x = hid[...].astype(jnp.float32)
    inv = lax.rsqrt(jnp.mean(x * x, axis=1, keepdims=True) + norm_eps)
    gains = gain[...].astype(jnp.float32).reshape(1, width)
    normed = (x * inv * gains).astype(jnp.bfloat16)
    lane = lax.broadcasted_iota(jnp.int32, (rows, LANES), 1)
    expert = lax.rem(lane, EXPERTS)
    routes = routes_v[...]
    weights = weights_v[...]
    weight = jnp.zeros((rows, LANES), jnp.float32)
    for k in range(routes.shape[1]):
        weight = weight + jnp.where(routes[:, k : k + 1] == expert, weights[:, k : k + 1], 0.0)
    high = weight.astype(jnp.bfloat16).astype(jnp.float32)
    tail = jnp.where(lane < EXPERTS, high, jnp.where(lane < 2 * EXPERTS, weight - high, 0.0))
    tail = tail.astype(jnp.bfloat16)
    count = ids_v.shape[1]
    ids = jnp.broadcast_to(ids_v[...].astype(jnp.float32), (rows, count)).astype(jnp.bfloat16)
    out_ref[:, :width] = normed
    out_ref[:, width : width + LANES] = tail
    out_ref[:, width + LANES : width + LANES + count] = ids


def merge_kernel(me_ref, own_ref, got_ref, out_ref, *, bit):
    rows = own_ref.shape[0]
    upper = (me_ref[0] & bit) != 0

    @pl.when(upper)
    def _():
        out_ref[:rows] = got_ref[...]
        out_ref[rows:] = own_ref[...]

    @pl.when(jnp.logical_not(upper))
    def _():
        out_ref[:rows] = own_ref[...]
        out_ref[rows:] = got_ref[...]


def load_kernel(src_ref, out_ref, sems, *, start):
    parts = sems.shape[0]
    step = out_ref.shape[0] // parts
    copies = [
        pltpu.make_async_copy(src_ref.at[pl.ds(start + i * step, step)], out_ref.at[pl.ds(i * step, step)], sems.at[i])
        for i in range(parts)
    ]
    for c in copies:
        c.start()
    for c in copies:
        c.wait()


def expert_kernel(*refs, tk, tn, base, rows, slices, role_size, loads):
    me_ref, xa_ref, xb_ref = refs[:3]
    pre_refs = refs[3 : 3 + loads]
    g_ref, u_ref, d_ref, pool_ref, keep_ref, send_ref, page_ref = refs[3 + loads : 10 + loads]
    gb, ub, db, ga, ua, h, wsel, vec, ids, semg, semu, semd, semi, semp = refs[10 + loads :]
    width = d_ref.shape[1]
    n1, n2 = width // tk, width // tn
    ready = sum(r.shape[0] for r in pre_refs) // tk
    nb, nd, ng = ub.shape[0], db.shape[0], gb.shape[0]
    half = xa_ref.shape[0]
    me = me_ref[0]

    def cg(i):
        s = lax.rem(i - ready, ng)
        return pltpu.make_async_copy(g_ref.at[pl.ds(i * tk, tk)], gb.at[s], semg.at[s])

    def cu(i):
        s = lax.rem(i, nb)
        return pltpu.make_async_copy(u_ref.at[pl.ds(i * tk, tk)], ub.at[s], semu.at[s])

    def cd(j):
        s = lax.rem(j, nd)
        cols = pl.ds(pl.multiple_of(j * tn, tn), tn)
        return pltpu.make_async_copy(d_ref.at[:, cols], db.at[s], semd.at[s])

    for i in range(ready, min(ready + ng, n1)):
        cg(i).start()
    for i in range(min(nb, n1)):
        cu(i).start()
    cols = vec.shape[1]
    vec[:half] = xa_ref[:, base : base + cols].astype(jnp.float32).astype(jnp.int32)
    vec[half:] = xb_ref[:, base : base + cols].astype(jnp.float32).astype(jnp.int32)
    move = pltpu.make_async_copy(vec, ids, semi)
    move.start()

    ga[...] = jnp.zeros_like(ga)
    ua[...] = jnp.zeros_like(ua)
    expert = me // slices
    lane = lax.broadcasted_iota(jnp.int32, (half, LANES), 1)
    chosen = (lane == expert) | (lane == expert + EXPERTS)
    for i, ref in enumerate((xa_ref, xb_ref)):
        tail = ref[:, width : width + LANES].astype(jnp.float32)
        wsel[i * half : (i + 1) * half] = jnp.sum(jnp.where(chosen, tail, 0.0), axis=1, keepdims=True)

    def rows_of(i):
        at = pl.ds(pl.multiple_of(i * tk, tk), tk)
        return jnp.concatenate([xa_ref[:, at], xb_ref[:, at]], axis=0)

    first = 0
    for ref in pre_refs:
        count = ref.shape[0] // tk

        def early(i, c, ref=ref, first=first):
            at = pl.ds(pl.multiple_of((i - first) * tk, tk), tk)
            ga[...] += jnp.dot(rows_of(i), ref[at, :], preferred_element_type=jnp.float32)
            return c

        lax.fori_loop(first, first + count, early, 0)
        first += count

    move.wait()
    count = page_ref.shape[0]
    peers = count // role_size
    bits = peers.bit_length() - 1
    mine = me // peers

    def page_start(d, c):
        other = d // peers != mine
        within = lax.rem(d, peers)
        block = jnp.int32(0)
        for b in range(bits):
            block = block * 2 + (lax.shift_right_logical(within, jnp.int32(b)) & 1)
        row = block * rows + jnp.where(other, half, 0)
        pltpu.make_async_copy(pool_ref.at[ids[row, me]], page_ref.at[d], semp.at[d]).start()
        return c

    def page_wait(d, c):
        pltpu.make_async_copy(pool_ref.at[0], page_ref.at[d], semp.at[d]).wait()
        return c

    lax.fori_loop(0, count, page_start, 0)

    def late(i, c):
        cg(i).wait()
        ga[...] += jnp.dot(rows_of(i), gb[lax.rem(i - ready, ng)], preferred_element_type=jnp.float32)

        @pl.when(i + ng < n1)
        def _():
            cg(i + ng).start()

        return c

    def up(i, c):
        cu(i).wait()
        ua[...] += jnp.dot(rows_of(i), ub[lax.rem(i, nb)], preferred_element_type=jnp.float32)

        @pl.when(i + nb < n1)
        def _():
            cu(i + nb).start()

        @pl.when((i + nd >= n1) & (i + nd - n1 < n2))
        def _():
            cd(i + nd - n1).start()

        return c

    lax.fori_loop(ready, n1, late, 0)
    lax.fori_loop(0, n1, up, 0)
    g = ga[...]
    h[...] = ((g / (1.0 + jnp.exp(-g))) * ua[...]).astype(jnp.bfloat16)

    def down(j, c):
        cd(j).wait()
        at = pl.ds(pl.multiple_of(j * tn, tn), tn)
        out = jnp.dot(h[...], db[lax.rem(j, nd)], preferred_element_type=jnp.float32)
        out = out * wsel[...]
        keep_ref[:, at] = out[:half]
        send_ref[:, at] = out[half:].astype(jnp.bfloat16)

        @pl.when(j + nd < n2)
        def _():
            cd(j + nd).start()

        return c

    lax.fori_loop(0, n2, down, 0)
    lax.fori_loop(0, count, page_wait, 0)


def attention_kernel(len_ref, owner_ref, q_ref, local_ref, page_ref, out_ref):
    requests, heads, width = q_ref.shape
    value = out_ref.shape[2]
    local_len = local_ref.shape[1]
    pages, page_len, _ = page_ref.shape
    paged = page_ref[...].reshape(pages * page_len, width)
    row = lax.broadcasted_iota(jnp.int32, (pages, pages * page_len), 0)
    col = lax.broadcasted_iota(jnp.int32, (pages, pages * page_len), 1)
    inside = (col >= row * page_len) & (col < (row + 1) * page_len)
    owner = jnp.broadcast_to(jnp.transpose(owner_ref[...].astype(jnp.float32)), inside.shape)
    key_owner = jnp.sum(jnp.where(inside, owner, 0.0), axis=0, keepdims=True)
    nt = (((1,), (1,)), ((), ()))
    for r in range(requests):
        q = q_ref[r]
        local = local_ref[r]
        s_local = lax.dot_general(q, local, nt, preferred_element_type=jnp.float32) * score_scale
        pos = lax.broadcasted_iota(jnp.int32, (heads, local_len), 1)
        s_local = jnp.where(pos < len_ref[r], s_local, -jnp.inf)
        s_page = lax.dot_general(q, paged, nt, preferred_element_type=jnp.float32) * score_scale
        s_page = jnp.where(key_owner == float(r), s_page, -jnp.inf)
        peak = jnp.maximum(jnp.max(s_local, axis=1, keepdims=True), jnp.max(s_page, axis=1, keepdims=True))
        e_local = jnp.exp(s_local - peak)
        e_page = jnp.exp(s_page - peak)
        total = jnp.sum(e_local, axis=1, keepdims=True) + jnp.sum(e_page, axis=1, keepdims=True)
        p_local = (e_local / total).astype(jnp.bfloat16)
        p_page = (e_page / total).astype(jnp.bfloat16)
        out = jnp.dot(p_local, local[:, :value], preferred_element_type=jnp.float32)
        out = out + jnp.dot(p_page, paged[:, :value], preferred_element_type=jnp.float32)
        out_ref[r] = out.astype(jnp.bfloat16)


def tile_of(size, want):
    tile = min(size, want)
    while size % tile:
        tile -= LANES
    return tile


def per_device(
    hidden, norm_gain, routes, gate_weights, w_gate, w_up, w_down,
    queries, local_cache, cache_lengths, swap_pool, page_ids, page_owner,
):
    role_size, dev_size = lax.axis_size("role"), lax.axis_size("dev")
    devices = role_size * dev_size
    slices = devices // EXPERTS
    me = lax.axis_index("role") * dev_size + lax.axis_index("dev")
    me_arr = jnp.reshape(me, (1,)).astype(jnp.int32)
    rows, width = hidden.shape
    units = w_gate.shape[1]
    id_cols = pl.cdiv(devices, LANES) * LANES
    packed_width = width + LANES + id_cols
    half = dev_size * rows
    total_rows = role_size * half
    tk = tn = tile_of(width, 512)
    weight_bytes = 2 * width * units
    bits = [dev_size >> (k + 1) for k in range(dev_size.bit_length() - 1)]
    weights_in = [pltpu.with_memory_space_constraint(w, pltpu.HBM) for w in (w_gate, w_up, w_down)]
    pool_in = pltpu.with_memory_space_constraint(swap_pool, pltpu.HBM)
    small_in = [
        pltpu.with_memory_space_constraint(a, pltpu.HBM)
        for a in (hidden, norm_gain, routes, gate_weights, page_ids)
    ]

    held = pl.pallas_call(
        pack_kernel,
        out_shape=jax.ShapeDtypeStruct((rows, packed_width), jnp.bfloat16),
        in_specs=[SM] + [HBM] * 5,
        out_specs=VM,
        scratch_shapes=[
            pltpu.VMEM(hidden.shape, hidden.dtype),
            pltpu.VMEM(norm_gain.shape, norm_gain.dtype),
            pltpu.VMEM(routes.shape, routes.dtype),
            pltpu.VMEM(gate_weights.shape, gate_weights.dtype),
            pltpu.VMEM(page_ids.shape, page_ids.dtype),
            pltpu.SemaphoreType.DMA((5,)),
        ],
        compiler_params=pltpu.CompilerParams(vmem_limit_bytes=6 << 20),
    )(me_arr, *small_in)

    def load(index, start):
        size = LOADS[index] * tk
        return pl.pallas_call(
            functools.partial(load_kernel, start=start),
            out_shape=pltpu.VMEM((size, units), jnp.bfloat16),
            in_specs=[HBM],
            out_specs=VM,
            scratch_shapes=[pltpu.SemaphoreType.DMA((LOADS[index],))],
            compiler_params=pltpu.CompilerParams(vmem_limit_bytes=1 << 20),
            cost_estimate=pl.CostEstimate(flops=0, bytes_accessed=2 * size * units, transcendentals=0),
        )(weights_in[0])

    loaded = []
    taken = 0
    for k, bit in enumerate(bits):
        got = lax.ppermute(held, "dev", [(i, i ^ bit) for i in range(dev_size)])
        if k < len(LOADS) - 1:
            loaded.append(load(k, taken))
            taken += LOADS[k] * tk
        held = pl.pallas_call(
            functools.partial(merge_kernel, bit=bit),
            out_shape=jax.ShapeDtypeStruct((2 * held.shape[0], packed_width), jnp.bfloat16),
            in_specs=[SM, VM, VM],
            out_specs=VM,
            compiler_params=pltpu.CompilerParams(vmem_limit_bytes=6 << 20),
        )(me_arr, held, got)
    other = role_swap(held)
    loaded.append(load(len(LOADS) - 1, taken))

    keep, send, outgoing = pl.pallas_call(
        functools.partial(
            expert_kernel, tk=tk, tn=tn, base=width + LANES, rows=rows, slices=slices,
            role_size=role_size, loads=len(loaded),
        ),
        out_shape=(
            jax.ShapeDtypeStruct((half, width), jnp.float32),
            jax.ShapeDtypeStruct((half, width), jnp.bfloat16),
            jax.ShapeDtypeStruct((devices,) + swap_pool.shape[1:], jnp.bfloat16),
        ),
        in_specs=[SM, VM, VM] + [VM] * len(loaded) + [HBM] * 4,
        out_specs=(VM, VM, VM),
        scratch_shapes=[
            pltpu.VMEM((GATE_SLOTS, tk, units), jnp.bfloat16),
            pltpu.VMEM((UP_SLOTS, tk, units), jnp.bfloat16),
            pltpu.VMEM((DOWN_SLOTS, units, tn), jnp.bfloat16),
            pltpu.VMEM((total_rows, units), jnp.float32),
            pltpu.VMEM((total_rows, units), jnp.float32),
            pltpu.VMEM((total_rows, units), jnp.bfloat16),
            pltpu.VMEM((total_rows, 1), jnp.float32),
            pltpu.VMEM((total_rows, id_cols), jnp.int32),
            pltpu.SMEM((total_rows, id_cols), jnp.int32),
            pltpu.SemaphoreType.DMA((GATE_SLOTS,)),
            pltpu.SemaphoreType.DMA((UP_SLOTS,)),
            pltpu.SemaphoreType.DMA((DOWN_SLOTS,)),
            pltpu.SemaphoreType.DMA,
            pltpu.SemaphoreType.DMA((devices,)),
        ],
        compiler_params=pltpu.CompilerParams(vmem_limit_bytes=32 << 20),
        cost_estimate=pl.CostEstimate(
            flops=6 * total_rows * width * units, bytes_accessed=3 * weight_bytes, transcendentals=0
        ),
    )(me_arr, held, other, *loaded, *weights_in, pool_in)

    crossed = role_swap(send)
    arrived = lax.all_to_all(outgoing, ("role", "dev"), split_axis=0, concat_axis=0, tiled=True)

    attn_out = pl.pallas_call(
        attention_kernel,
        out_shape=jax.ShapeDtypeStruct(queries.shape[:2] + (queries.shape[2] - ROPE,), jnp.bfloat16),
        in_specs=[SM, VM, VM, VM, VM],
        out_specs=VM,
        compiler_params=pltpu.CompilerParams(vmem_limit_bytes=20 << 20),
        cost_estimate=pl.CostEstimate(flops=1 << 27, bytes_accessed=1 << 20, transcendentals=1 << 16),
    )(cache_lengths, page_owner, queries, local_cache, arrived)

    total = (keep + crossed.astype(jnp.float32)).astype(jnp.bfloat16)
    count = len(bits)
    total = total.reshape((2,) * count + (rows, width))
    total = total.transpose(tuple(range(count - 1, -1, -1)) + (count, count + 1)).reshape(dev_size, rows, width)
    parts = lax.all_to_all(total, "dev", split_axis=0, concat_axis=0, tiled=True)
    total = jnp.sum(parts.astype(jnp.float32), axis=0)
    moe_out = (hidden.astype(jnp.float32) + total).astype(jnp.bfloat16)
    return (attn_out, moe_out)


def solution(mesh):
    in_specs = (
        P(("group", "role", "dev"), None),
        P(),
        P(("group", "role", "dev"), None),
        P(("group", "role", "dev"), None),
        P(None, ("role", "dev")),
        P(None, ("role", "dev")),
        P(("role", "dev"), None),
        P(("group", "role", "dev"), None, None),
        P(("group", "role", "dev"), None, None),
        P(("group", "role", "dev")),
        P(("group", "role", "dev"), None, None),
        P(("group", "role", "dev"), None),
        P(("group", "role", "dev"), None),
    )
    out_specs = (P(("group", "role", "dev"), None, None), P(("group", "role", "dev"), None))
    return jax.shard_map(per_device, mesh=mesh, in_specs=in_specs, out_specs=out_specs, check_vma=False)
```

```python
import functools

import jax
import jax.numpy as jnp
from jax import lax
from jax.experimental import pallas as pl
from jax.experimental.pallas import tpu as pltpu
from jax.sharding import PartitionSpec as P


ROPE = 64
EXPERTS = 16
LANES = 128

LOADS = (3, 3, 2)
GATE_SLOTS = 4
UP_SLOTS = 5
DOWN_SLOTS = 5

score_scale = 192.0 ** (-0.5)
norm_eps = 1e-06


VM = pl.BlockSpec(memory_space=pltpu.VMEM)
SM = pl.BlockSpec(memory_space=pltpu.SMEM)
HBM = pl.BlockSpec(memory_space=pltpu.HBM)


def role_swap(x):
    size = lax.axis_size("role")
    return lax.ppermute(x, "role", [(i, size - 1 - i) for i in range(size)])


def pack_kernel(me_ref, hid_ref, gain_ref, routes_ref, weights_ref, ids_ref, out_ref, hid, gain, routes_v, weights_v, ids_v, sems):
    rows, width = hid.shape
    copies = [
        pltpu.make_async_copy(src, dst, sems.at[i])
        for i, (src, dst) in enumerate(
            ((hid_ref, hid), (gain_ref, gain), (routes_ref, routes_v), (weights_ref, weights_v), (ids_ref, ids_v))
        )
    ]
    for c in copies:
        c.start()
    for c in copies:
        c.wait()
    x = hid[...].astype(jnp.float32)
    inv = lax.rsqrt(jnp.mean(x * x, axis=1, keepdims=True) + norm_eps)
    gains = gain[...].astype(jnp.float32).reshape(1, width)
    normed = (x * inv * gains).astype(jnp.bfloat16)
    lane = lax.broadcasted_iota(jnp.int32, (rows, LANES), 1)
    expert = lax.rem(lane, EXPERTS)
    routes = routes_v[...]
    weights = weights_v[...]
    weight = jnp.zeros((rows, LANES), jnp.float32)
    for k in range(routes.shape[1]):
        weight = weight + jnp.where(routes[:, k : k + 1] == expert, weights[:, k : k + 1], 0.0)
    high = weight.astype(jnp.bfloat16).astype(jnp.float32)
    tail = jnp.where(lane < EXPERTS, high, jnp.where(lane < 2 * EXPERTS, weight - high, 0.0))
    tail = tail.astype(jnp.bfloat16)
    count = ids_v.shape[1]
    ids = jnp.broadcast_to(ids_v[...].astype(jnp.float32), (rows, count)).astype(jnp.bfloat16)
    out_ref[:, :width] = normed
    out_ref[:, width : width + LANES] = tail
    out_ref[:, width + LANES : width + LANES + count] = ids


def bit_groups(size):
    groups = []
    top = size.bit_length() - 1
    while top > 0:
        length = min(2, top)
        top -= length
        groups.append((top, 1 << length))
    return groups


def block_of(index, groups):
    block = 0
    for low, members in reversed(groups):
        block = block * members + ((index >> low) & (members - 1))
    return block


def merge_kernel(me_ref, *refs, low):
    members = len(refs) - 1
    out_ref = refs[-1]
    rows = refs[0].shape[0]
    mine = (me_ref[0] >> low) & (members - 1)
    for place in range(members):

        @pl.when(mine == place)
        def _(place=place):
            for offset in range(members):
                at = (place ^ offset) * rows
                out_ref[at : at + rows] = refs[offset][...]


def load_kernel(src_ref, out_ref, sems, *, start):
    parts = sems.shape[0]
    step = out_ref.shape[0] // parts
    copies = [
        pltpu.make_async_copy(src_ref.at[pl.ds(start + i * step, step)], out_ref.at[pl.ds(i * step, step)], sems.at[i])
        for i in range(parts)
    ]
    for c in copies:
        c.start()
    for c in copies:
        c.wait()


def expert_kernel(*refs, tk, tn, base, rows, slices, groups, loads):
    me_ref, xa_ref, xb_ref = refs[:3]
    pre_refs = refs[3 : 3 + loads]
    g_ref, u_ref, d_ref, pool_ref, keep_ref, send_ref, near_ref, far_ref = refs[3 + loads : 11 + loads]
    gb, ub, db, ga, ua, h, wsel, vec, ids, semg, semu, semd, semi, semp = refs[11 + loads :]
    width = d_ref.shape[1]
    n1, n2 = width // tk, width // tn
    ready = sum(r.shape[0] for r in pre_refs) // tk
    nb, nd, ng = ub.shape[0], db.shape[0], gb.shape[0]
    half = xa_ref.shape[0]
    me = me_ref[0]

    def cg(i):
        s = lax.rem(i - ready, ng)
        return pltpu.make_async_copy(g_ref.at[pl.ds(i * tk, tk)], gb.at[s], semg.at[s])

    def cu(i):
        s = lax.rem(i, nb)
        return pltpu.make_async_copy(u_ref.at[pl.ds(i * tk, tk)], ub.at[s], semu.at[s])

    def cd(j):
        s = lax.rem(j, nd)
        cols = pl.ds(pl.multiple_of(j * tn, tn), tn)
        return pltpu.make_async_copy(d_ref.at[:, cols], db.at[s], semd.at[s])

    for i in range(min(nb, n1)):
        cu(i).start()
    for i in range(ready, min(ready + ng, n1)):
        cg(i).start()
    cols = vec.shape[1]
    vec[:half] = xa_ref[:, base : base + cols].astype(jnp.float32).astype(jnp.int32)
    vec[half:] = xb_ref[:, base : base + cols].astype(jnp.float32).astype(jnp.int32)
    move = pltpu.make_async_copy(vec, ids, semi)
    move.start()

    ga[...] = jnp.zeros_like(ga)
    ua[...] = jnp.zeros_like(ua)
    expert = me // slices
    lane = lax.broadcasted_iota(jnp.int32, (half, LANES), 1)
    chosen = (lane == expert) | (lane == expert + EXPERTS)
    for i, ref in enumerate((xa_ref, xb_ref)):
        tail = ref[:, width : width + LANES].astype(jnp.float32)
        wsel[i * half : (i + 1) * half] = jnp.sum(jnp.where(chosen, tail, 0.0), axis=1, keepdims=True)

    def rows_of(i):
        at = pl.ds(pl.multiple_of(i * tk, tk), tk)
        return jnp.concatenate([xa_ref[:, at], xb_ref[:, at]], axis=0)

    def up(i, xs):
        cu(i).wait()
        ua[...] += jnp.dot(xs, ub[lax.rem(i, nb)], preferred_element_type=jnp.float32)

        @pl.when(i + nb < n1)
        def _():
            cu(i + nb).start()

        @pl.when((i + nd >= n1) & (i + nd - n1 < n2))
        def _():
            cd(i + nd - n1).start()

    peers = near_ref.shape[0]

    def page_start(d):
        row = block_of(d, groups) * rows
        for n, ref in enumerate((near_ref, far_ref)):
            page = pool_ref.at[ids[row + n * half, me]]
            pltpu.make_async_copy(page, ref.at[d], semp.at[n]).start()

    first = 0
    for n, ref in enumerate(pre_refs):
        size = ref.shape[0] // tk

        def early(i, c, ref=ref, first=first):
            at = pl.ds(pl.multiple_of((i - first) * tk, tk), tk)
            xs = rows_of(i)
            ga[...] += jnp.dot(xs, ref[at, :], preferred_element_type=jnp.float32)
            up(i, xs)
            return c

        lax.fori_loop(first, first + size, early, 0)
        first += size
        if n == 0:
            move.wait()
            for d in range(peers):
                page_start(d)

    def late(i, c):
        cg(i).wait()
        xs = rows_of(i)
        ga[...] += jnp.dot(xs, gb[lax.rem(i - ready, ng)], preferred_element_type=jnp.float32)

        @pl.when(i + ng < n1)
        def _():
            cg(i + ng).start()

        up(i, xs)
        return c

    lax.fori_loop(ready, n1, late, 0)
    g = ga[...]
    h[...] = ((g / (1.0 + jnp.exp(-g))) * ua[...]).astype(jnp.bfloat16)

    def down(j, c):
        cd(j).wait()
        at = pl.ds(pl.multiple_of(j * tn, tn), tn)
        out = jnp.dot(h[...], db[lax.rem(j, nd)], preferred_element_type=jnp.float32)
        out = out * wsel[...]
        keep_ref[:, at] = out[:half]
        send_ref[:, at] = out[half:].astype(jnp.bfloat16)

        @pl.when(j + nd < n2)
        def _():
            cd(j + nd).start()

        return c

    lax.fori_loop(0, n2, down, 0)
    for n, ref in enumerate((near_ref, far_ref)):
        pltpu.make_async_copy(ref, ref, semp.at[n]).wait()


def fold_kernel(me_ref, *refs, low, members, arrived):
    own_ref, got_refs = refs[0], refs[1 : 1 + arrived]
    keep_ref, send_refs = refs[1 + arrived], refs[2 + arrived :]
    rows = keep_ref.shape[0]
    mine = (me_ref[0] >> low) & (members - 1)

    def block(place):
        at = slice(place * rows, (place + 1) * rows)
        total = own_ref[at]
        for ref in got_refs:
            total = total + ref[at].astype(jnp.float32)
        return total

    for place in range(members):

        @pl.when(mine == place)
        def _(place=place):
            for offset in range(1, members):
                send_refs[offset - 1][...] = block(place ^ offset).astype(jnp.bfloat16)
            keep_ref[...] = block(place)


def stack_kernel(near_ref, far_ref, out_ref):
    page = near_ref.shape[1]
    out_ref[:, :page] = near_ref[...]
    out_ref[:, page:] = far_ref[...]


def finish_kernel(me_ref, len_ref, owner_ref, q_ref, local_ref, page_ref, hid_ref, own_ref, *refs):
    got_refs, out_ref, moe_ref = refs[:-2], refs[-2], refs[-1]
    total = own_ref[...]
    for ref in got_refs:
        total = total + ref[...].astype(jnp.float32)
    moe_ref[...] = (hid_ref[...].astype(jnp.float32) + total).astype(jnp.bfloat16)

    requests, heads, width = q_ref.shape
    value = out_ref.shape[2]
    local_len = local_ref.shape[1]
    peers, both, _ = page_ref.shape
    page_len = both // 2
    devices = owner_ref.shape[1]
    role = me_ref[0] // peers
    keys = page_ref[...].reshape(peers * both, width)
    holder = lax.broadcasted_iota(jnp.int32, (devices, peers * both), 0)
    col = lax.broadcasted_iota(jnp.int32, (devices, peers * both), 1)
    source = col // both
    far = (col - source * both) // page_len
    sender = jnp.where(far == 0, role, devices // peers - 1 - role) * peers + source
    owner = jnp.broadcast_to(jnp.transpose(owner_ref[...].astype(jnp.float32)), holder.shape)
    key_owner = jnp.sum(jnp.where(holder == sender, owner, 0.0), axis=0, keepdims=True)
    nt = (((1,), (1,)), ((), ()))
    queries = q_ref[...].reshape(requests * heads, width)
    s_page = lax.dot_general(queries, keys, nt, preferred_element_type=jnp.float32) * score_scale
    request = (lax.broadcasted_iota(jnp.int32, s_page.shape, 0) // heads).astype(jnp.float32)
    s_page = jnp.where(key_owner == request, s_page, -jnp.inf)
    pos = lax.broadcasted_iota(jnp.int32, (heads, local_len), 1)
    s_local = []
    for r in range(requests):
        s = lax.dot_general(q_ref[r], local_ref[r], nt, preferred_element_type=jnp.float32) * score_scale
        s_local.append(jnp.where(pos < len_ref[r], s, -jnp.inf))
    s_local = jnp.concatenate(s_local, axis=0)
    peak = jnp.maximum(jnp.max(s_local, axis=1, keepdims=True), jnp.max(s_page, axis=1, keepdims=True))
    e_local = jnp.exp(s_local - peak)
    e_page = jnp.exp(s_page - peak)
    norm = jnp.sum(e_local, axis=1, keepdims=True) + jnp.sum(e_page, axis=1, keepdims=True)
    p_local = (e_local / norm).astype(jnp.bfloat16)
    p_page = (e_page / norm).astype(jnp.bfloat16)
    paged = jnp.dot(p_page, keys[:, :value], preferred_element_type=jnp.float32)
    for r in range(requests):
        at = slice(r * heads, (r + 1) * heads)
        out = jnp.dot(p_local[at], local_ref[r][:, :value], preferred_element_type=jnp.float32)
        out_ref[r] = (out + paged[at]).astype(jnp.bfloat16)


def tile_of(size, want):
    tile = min(size, want)
    while size % tile:
        tile -= LANES
    return tile


def per_device(
    hidden, norm_gain, routes, gate_weights, w_gate, w_up, w_down,
    queries, local_cache, cache_lengths, swap_pool, page_ids, page_owner,
):
    role_size, dev_size = lax.axis_size("role"), lax.axis_size("dev")
    devices = role_size * dev_size
    slices = devices // EXPERTS
    me = lax.axis_index("role") * dev_size + lax.axis_index("dev")
    me_arr = jnp.reshape(me, (1,)).astype(jnp.int32)
    rows, width = hidden.shape
    units = w_gate.shape[1]
    id_cols = pl.cdiv(devices, LANES) * LANES
    packed_width = width + LANES + id_cols
    half = dev_size * rows
    total_rows = role_size * half
    tk = tn = tile_of(width, 512)
    weight_bytes = 2 * width * units
    groups = bit_groups(dev_size)
    weights_in = [pltpu.with_memory_space_constraint(w, pltpu.HBM) for w in (w_gate, w_up, w_down)]
    pool_in = pltpu.with_memory_space_constraint(swap_pool, pltpu.HBM)
    small_in = [
        pltpu.with_memory_space_constraint(a, pltpu.HBM)
        for a in (hidden, norm_gain, routes, gate_weights, page_ids)
    ]

    held = pl.pallas_call(
        pack_kernel,
        out_shape=jax.ShapeDtypeStruct((rows, packed_width), jnp.bfloat16),
        in_specs=[SM] + [HBM] * 5,
        out_specs=VM,
        scratch_shapes=[
            pltpu.VMEM(hidden.shape, hidden.dtype),
            pltpu.VMEM(norm_gain.shape, norm_gain.dtype),
            pltpu.VMEM(routes.shape, routes.dtype),
            pltpu.VMEM(gate_weights.shape, gate_weights.dtype),
            pltpu.VMEM(page_ids.shape, page_ids.dtype),
            pltpu.SemaphoreType.DMA((5,)),
        ],
        compiler_params=pltpu.CompilerParams(vmem_limit_bytes=6 << 20),
    )(me_arr, *small_in)

    def load(index, start):
        size = LOADS[index] * tk
        return pl.pallas_call(
            functools.partial(load_kernel, start=start),
            out_shape=pltpu.VMEM((size, units), jnp.bfloat16),
            in_specs=[HBM],
            out_specs=VM,
            scratch_shapes=[pltpu.SemaphoreType.DMA((LOADS[index],))],
            compiler_params=pltpu.CompilerParams(vmem_limit_bytes=1 << 20),
            cost_estimate=pl.CostEstimate(flops=0, bytes_accessed=2 * size * units, transcendentals=0),
        )(weights_in[0])

    def swap(value, offset):
        return lax.ppermute(value, "dev", [(i, i ^ offset) for i in range(dev_size)])

    loaded = []
    taken = 0
    for k, (low, members) in enumerate(groups):
        got = [swap(held, offset << low) for offset in range(1, members)]
        if k < len(LOADS) - 1:
            loaded.append(load(k, taken))
            taken += LOADS[k] * tk
        held = pl.pallas_call(
            functools.partial(merge_kernel, low=low),
            out_shape=jax.ShapeDtypeStruct((members * held.shape[0], packed_width), jnp.bfloat16),
            in_specs=[SM] + [VM] * members,
            out_specs=VM,
            compiler_params=pltpu.CompilerParams(vmem_limit_bytes=6 << 20),
        )(me_arr, held, *got)
    other = role_swap(held)
    loaded.append(load(len(LOADS) - 1, taken))

    keep, send, near, far = pl.pallas_call(
        functools.partial(
            expert_kernel, tk=tk, tn=tn, base=width + LANES, rows=rows, slices=slices,
            groups=groups, loads=len(loaded),
        ),
        out_shape=(
            jax.ShapeDtypeStruct((half, width), jnp.float32),
            jax.ShapeDtypeStruct((half, width), jnp.bfloat16),
            jax.ShapeDtypeStruct((dev_size,) + swap_pool.shape[1:], jnp.bfloat16),
            jax.ShapeDtypeStruct((dev_size,) + swap_pool.shape[1:], jnp.bfloat16),
        ),
        in_specs=[SM, VM, VM] + [VM] * len(loaded) + [HBM] * 4,
        out_specs=(VM, VM, VM, VM),
        scratch_shapes=[
            pltpu.VMEM((GATE_SLOTS, tk, units), jnp.bfloat16),
            pltpu.VMEM((UP_SLOTS, tk, units), jnp.bfloat16),
            pltpu.VMEM((DOWN_SLOTS, units, tn), jnp.bfloat16),
            pltpu.VMEM((total_rows, units), jnp.float32),
            pltpu.VMEM((total_rows, units), jnp.float32),
            pltpu.VMEM((total_rows, units), jnp.bfloat16),
            pltpu.VMEM((total_rows, 1), jnp.float32),
            pltpu.VMEM((total_rows, id_cols), jnp.int32),
            pltpu.SMEM((total_rows, id_cols), jnp.int32),
            pltpu.SemaphoreType.DMA((GATE_SLOTS,)),
            pltpu.SemaphoreType.DMA((UP_SLOTS,)),
            pltpu.SemaphoreType.DMA((DOWN_SLOTS,)),
            pltpu.SemaphoreType.DMA,
            pltpu.SemaphoreType.DMA((2,)),
        ],
        compiler_params=pltpu.CompilerParams(vmem_limit_bytes=31 << 20),
        cost_estimate=pl.CostEstimate(
            flops=6 * total_rows * width * units, bytes_accessed=3 * weight_bytes, transcendentals=0
        ),
    )(me_arr, held, other, *loaded, *weights_in, pool_in)

    far = role_swap(far)
    page_shape = (dev_size, 2 * swap_pool.shape[1], swap_pool.shape[2])
    outgoing = pl.pallas_call(
        stack_kernel,
        out_shape=jax.ShapeDtypeStruct(page_shape, jnp.bfloat16),
        in_specs=[VM, VM],
        out_specs=VM,
        compiler_params=pltpu.CompilerParams(vmem_limit_bytes=8 << 20),
    )(near, far)
    arrived = lax.all_to_all(outgoing, "dev", split_axis=0, concat_axis=0, tiled=True)

    got = [role_swap(send)]
    own = keep
    for low, members in reversed(groups):
        count = own.shape[0] // members
        own, *sends = pl.pallas_call(
            functools.partial(fold_kernel, low=low, members=members, arrived=len(got)),
            out_shape=[jax.ShapeDtypeStruct((count, width), jnp.float32)]
            + [jax.ShapeDtypeStruct((count, width), jnp.bfloat16)] * (members - 1),
            in_specs=[SM] + [VM] * (1 + len(got)),
            out_specs=[VM] * members,
            compiler_params=pltpu.CompilerParams(vmem_limit_bytes=16 << 20),
        )(me_arr, own, *got)
        got = [swap(value, (n + 1) << low) for n, value in enumerate(sends)]
    operands = (me_arr, cache_lengths, page_owner, queries, local_cache, arrived, hidden, own, *got)
    attn_out, moe_out = pl.pallas_call(
        finish_kernel,
        out_shape=(
            jax.ShapeDtypeStruct(queries.shape[:2] + (queries.shape[2] - ROPE,), jnp.bfloat16),
            jax.ShapeDtypeStruct(hidden.shape, jnp.bfloat16),
        ),
        in_specs=[SM] * 2 + [VM] * (len(operands) - 2),
        out_specs=(VM, VM),
        compiler_params=pltpu.CompilerParams(vmem_limit_bytes=24 << 20),
    )(*operands)
    return (attn_out, moe_out)


def solution(mesh):
    in_specs = (
        P(("group", "role", "dev"), None),
        P(),
        P(("group", "role", "dev"), None),
        P(("group", "role", "dev"), None),
        P(None, ("role", "dev")),
        P(None, ("role", "dev")),
        P(("role", "dev"), None),
        P(("group", "role", "dev"), None, None),
        P(("group", "role", "dev"), None, None),
        P(("group", "role", "dev")),
        P(("group", "role", "dev"), None, None),
        P(("group", "role", "dev"), None),
        P(("group", "role", "dev"), None),
    )
    out_specs = (P(("group", "role", "dev"), None, None), P(("group", "role", "dev"), None))
    return jax.shard_map(per_device, mesh=mesh, in_specs=in_specs, out_specs=out_specs, check_vma=False)
```

```python
import functools

import jax
import jax.numpy as jnp
from jax import lax
from jax.experimental import pallas as pl
from jax.experimental.pallas import tpu as pltpu
from jax.sharding import PartitionSpec as P


ROPE = 64
EXPERTS = 16
LANES = 128

LOADS = (2, 2)
LEAD = 2
GATE_SLOTS = 2
UP_SLOTS = 3
DOWN_SLOTS = 6

score_scale = 192.0 ** (-0.5)
norm_eps = 1e-06


VM = pl.BlockSpec(memory_space=pltpu.VMEM)
SM = pl.BlockSpec(memory_space=pltpu.SMEM)
HBM = pl.BlockSpec(memory_space=pltpu.HBM)


def role_swap(x):
    size = lax.axis_size("role")
    return lax.ppermute(x, "role", [(i, size - 1 - i) for i in range(size)])


def pack_kernel(me_ref, hid_ref, gain_ref, routes_ref, weights_ref, ids_ref, out_ref, hid, gain, routes_v, weights_v, ids_v, sems):
    rows, width = hid.shape
    copies = [
        pltpu.make_async_copy(src, dst, sems.at[i])
        for i, (src, dst) in enumerate(
            ((hid_ref, hid), (gain_ref, gain), (routes_ref, routes_v), (weights_ref, weights_v), (ids_ref, ids_v))
        )
    ]
    for c in copies:
        c.start()
    for c in copies:
        c.wait()
    x = hid[...].astype(jnp.float32)
    inv = lax.rsqrt(jnp.mean(x * x, axis=1, keepdims=True) + norm_eps)
    gains = gain[...].astype(jnp.float32).reshape(1, width)
    normed = (x * inv * gains).astype(jnp.bfloat16)
    lane = lax.broadcasted_iota(jnp.int32, (rows, LANES), 1)
    expert = lax.rem(lane, EXPERTS)
    routes = routes_v[...]
    weights = weights_v[...]
    weight = jnp.zeros((rows, LANES), jnp.float32)
    for k in range(routes.shape[1]):
        weight = weight + jnp.where(routes[:, k : k + 1] == expert, weights[:, k : k + 1], 0.0)
    high = weight.astype(jnp.bfloat16).astype(jnp.float32)
    tail = jnp.where(lane < EXPERTS, high, jnp.where(lane < 2 * EXPERTS, weight - high, 0.0))
    tail = tail.astype(jnp.bfloat16)
    count = ids_v.shape[1]
    ids = jnp.broadcast_to(ids_v[...].astype(jnp.float32), (rows, count)).astype(jnp.bfloat16)
    out_ref[:, :width] = normed
    out_ref[:, width : width + LANES] = tail
    out_ref[:, width + LANES :] = jnp.zeros((rows, out_ref.shape[1] - width - LANES), jnp.bfloat16)
    out_ref[:, width + LANES : width + LANES + count] = ids


def bit_groups(size):
    groups = []
    top = size.bit_length() - 1
    while top > 0:
        length = min(2, top)
        top -= length
        groups.append((top, 1 << length))
    return groups


def block_of(index, groups):
    block = 0
    for low, members in reversed(groups):
        block = block * members + ((index >> low) & (members - 1))
    return block


def merge_kernel(me_ref, *refs, low):
    members = len(refs) - 1
    out_ref = refs[-1]
    rows = refs[0].shape[0]
    mine = (me_ref[0] >> low) & (members - 1)
    for place in range(members):

        @pl.when(mine == place)
        def _(place=place):
            for offset in range(members):
                at = (place ^ offset) * rows
                out_ref[at : at + rows] = refs[offset][...]


def load_kernel(src_ref, out_ref, sems, *, start):
    parts = sems.shape[0]
    step = out_ref.shape[0] // parts
    copies = [
        pltpu.make_async_copy(src_ref.at[pl.ds(start + i * step, step)], out_ref.at[pl.ds(i * step, step)], sems.at[i])
        for i in range(parts)
    ]
    for c in copies:
        c.start()
    for c in copies:
        c.wait()


def rows_of(xa_ref, xb_ref, i, tk):
    at = pl.ds(pl.multiple_of(i * tk, tk), tk)
    return jnp.concatenate([xa_ref[:, at], xb_ref[:, at]], axis=0)


def expert_kernel(*refs, tk, tn, base, rows, slices, groups, loads, parts):
    me_ref, xa_ref, xb_ref = refs[:3]
    pre_refs = refs[3 : 3 + loads]
    g_ref, u_ref, d_ref, pool_ref, keep_ref = refs[3 + loads : 8 + loads]
    send_refs = refs[8 + loads : 7 + loads + parts]
    near_ref, far_ref, gb, ub, db, ga, ua, h, wsel, vec, ids, semg, semu, semd, semi, semp = refs[7 + loads + parts :]
    width = d_ref.shape[1]
    n1, n2 = width // tk, width // tn
    ready = sum(r.shape[0] for r in pre_refs) // tk
    lead = min(LEAD, ready)
    nb, nd, ng = ub.shape[0], db.shape[0], gb.shape[0]
    half = xa_ref.shape[0]
    me = me_ref[0]

    def cg(i):
        s = lax.rem(i - ready, ng)
        return pltpu.make_async_copy(g_ref.at[pl.ds(i * tk, tk)], gb.at[s], semg.at[s])

    def cu(i):
        s = lax.rem(i, nb)
        return pltpu.make_async_copy(u_ref.at[pl.ds(i * tk, tk)], ub.at[s], semu.at[s])

    def cd(j):
        s = lax.rem(j, nd)
        cols = pl.ds(pl.multiple_of(j * tn, tn), tn)
        return pltpu.make_async_copy(d_ref.at[:, cols], db.at[s], semd.at[s])

    for i in range(min(nb, n1)):
        cu(i).start()
    for i in range(ready, min(ready + ng, n1)):
        cg(i).start()
    cols = vec.shape[1]
    vec[:half] = xa_ref[:, base : base + cols].astype(jnp.float32).astype(jnp.int32)
    vec[half:] = xb_ref[:, base : base + cols].astype(jnp.float32).astype(jnp.int32)
    move = pltpu.make_async_copy(vec, ids, semi)
    move.start()

    ga[...] = jnp.zeros_like(ga)
    ua[...] = jnp.zeros_like(ua)
    expert = me // slices
    lane = lax.broadcasted_iota(jnp.int32, (half, LANES), 1)
    chosen = (lane == expert) | (lane == expert + EXPERTS)
    for i, ref in enumerate((xa_ref, xb_ref)):
        tail = ref[:, width : width + LANES].astype(jnp.float32)
        wsel[i * half : (i + 1) * half] = jnp.sum(jnp.where(chosen, tail, 0.0), axis=1, keepdims=True)

    peers = near_ref.shape[0]

    def page_start(d):
        row = block_of(d, groups) * rows
        for n, ref in enumerate((near_ref, far_ref)):
            page = pool_ref.at[ids[row + n * half, me]]
            pltpu.make_async_copy(page, ref.at[d], semp.at[n]).start()

    def gate(i, weights):
        ga[...] += jnp.dot(rows_of(xa_ref, xb_ref, i, tk), weights, preferred_element_type=jnp.float32)

    def up(i):
        cu(i).wait()
        xs = rows_of(xa_ref, xb_ref, i, tk)
        ua[...] += jnp.dot(xs, ub[lax.rem(i, nb)], preferred_element_type=jnp.float32)

        @pl.when(i + nb < n1)
        def _():
            cu(i + nb).start()

        @pl.when((i + nd >= n1) & (i + nd - n1 < n2))
        def _():
            cd(i + nd - n1).start()

    for j in range(min(n2, max(0, nd - n1))):
        cd(j).start()
    step = 0
    for ref in pre_refs:
        for k in range(ref.shape[0] // tk):
            gate(step, ref[k * tk : (k + 1) * tk, :])
            if step == 0:
                move.wait()
                for d in range(peers):
                    page_start(d)
            if step >= lead:
                up(step - lead)
            step += 1

    def late(i, c):
        cg(i).wait()
        gate(i, gb[lax.rem(i - ready, ng)])

        @pl.when(i + ng < n1)
        def _():
            cg(i + ng).start()

        up(i - lead)
        return c

    def rest(i, c):
        up(i)
        return c

    lax.fori_loop(ready, n1, late, 0)
    lax.fori_loop(n1 - lead, n1, rest, 0)
    g = ga[...]
    h[...] = ((g / (1.0 + jnp.exp(-g))) * ua[...]).astype(jnp.bfloat16)

    low, members = groups[-1]
    place = (me >> low) & (members - 1)
    size = half // members

    def down(j, c):
        cd(j).wait()
        at = pl.ds(pl.multiple_of(j * tn, tn), tn)
        out = jnp.dot(h[...], db[lax.rem(j, nd)], preferred_element_type=jnp.float32)
        out = out * wsel[...]
        for n, ref in enumerate((keep_ref,) + tuple(send_refs)):
            start = (n // members) * half
            want = place ^ (n % members)
            block = out[start : start + size]
            for p in range(1, members):
                block = jnp.where(want == p, out[start + p * size : start + (p + 1) * size], block)
            ref[:, at] = block.astype(ref.dtype)

        @pl.when(j + nd < n2)
        def _():
            cd(j + nd).start()

        return c

    lax.fori_loop(0, n2, down, 0, unroll=2)
    for n, ref in enumerate((near_ref, far_ref)):
        pltpu.make_async_copy(ref, ref, semp.at[n]).wait()


def fold_kernel(me_ref, *refs, low, members, arrived):
    own_ref, got_refs = refs[0], refs[1 : 1 + arrived]
    keep_ref, send_refs = refs[1 + arrived], refs[2 + arrived :]
    rows = keep_ref.shape[0]
    mine = (me_ref[0] >> low) & (members - 1)

    def block(place):
        at = slice(place * rows, (place + 1) * rows)
        total = own_ref[at]
        for ref in got_refs:
            total = total + ref[at].astype(jnp.float32)
        return total

    for place in range(members):

        @pl.when(mine == place)
        def _(place=place):
            for offset in range(1, members):
                send_refs[offset - 1][...] = block(place ^ offset).astype(jnp.bfloat16)
            keep_ref[...] = block(place)


def stack_kernel(near_ref, far_ref, out_ref):
    width = near_ref.shape[2]
    value = width - ROPE
    for n, ref in enumerate((near_ref, far_ref)):
        out_ref[:, :, n * value : (n + 1) * value] = ref[:, :, :value]
        out_ref[:, :, 2 * value + n * ROPE : 2 * value + (n + 1) * ROPE] = ref[:, :, value:]


def early_kernel(me_ref, len_ref, owner_ref, q_ref, local_ref, bias_ref, score_ref):
    requests, heads, _ = q_ref.shape
    local_len = local_ref.shape[1]
    devices = owner_ref.shape[1]
    keys = bias_ref.shape[1]
    page_len = keys // devices
    half = devices // 2
    mine = me_ref[0] // half
    holder = lax.broadcasted_iota(jnp.int32, (devices, keys), 0)
    slot = lax.broadcasted_iota(jnp.int32, (devices, keys), 1) // page_len
    sender = jnp.where(mine == 0, slot, jnp.where(slot < half, slot + half, slot - half))
    owner = jnp.broadcast_to(jnp.transpose(owner_ref[...].astype(jnp.float32)), holder.shape)
    key_owner = jnp.sum(jnp.where(holder == sender, owner, 0.0), axis=0, keepdims=True)
    request = (lax.broadcasted_iota(jnp.int32, bias_ref.shape, 0) // heads).astype(jnp.float32)
    bias_ref[...] = jnp.where(key_owner == request, 0.0, -jnp.inf)
    pos = lax.broadcasted_iota(jnp.int32, (heads, local_len), 1)
    nt = (((1,), (1,)), ((), ()))
    for r in range(requests):
        s = lax.dot_general(q_ref[r], local_ref[r], nt, preferred_element_type=jnp.float32) * score_scale
        score_ref[r * heads : (r + 1) * heads] = jnp.where(pos < len_ref[r], s, -jnp.inf)


def finish_kernel(bias_ref, score_ref, q_ref, local_ref, page_ref, hid_ref, own_ref, *refs):
    got_refs, out_ref, moe_ref = refs[:-2], refs[-2], refs[-1]
    total = own_ref[...]
    for ref in got_refs:
        total = total + ref[...].astype(jnp.float32)
    moe_ref[...] = (hid_ref[...].astype(jnp.float32) + total).astype(jnp.bfloat16)

    requests, heads, width = q_ref.shape
    value = out_ref.shape[2]
    peers, page_len, _ = page_ref.shape

    def keys_of(start, size):
        part = page_ref[:, :, start : start + size]
        return part.reshape(peers * page_len, size)

    wide = jnp.concatenate([keys_of(0, value), keys_of(value, value)], axis=0)
    thin = jnp.concatenate([keys_of(2 * value, ROPE), keys_of(2 * value + ROPE, ROPE)], axis=0)
    nt = (((1,), (1,)), ((), ()))
    queries = q_ref[...].reshape(requests * heads, width)
    s_page = lax.dot_general(queries[:, :value], wide, nt, preferred_element_type=jnp.float32)
    s_page = s_page + lax.dot_general(queries[:, value:], thin, nt, preferred_element_type=jnp.float32)
    s_page = s_page * score_scale + bias_ref[...]
    s_local = score_ref[...]
    peak = jnp.maximum(jnp.max(s_local, axis=1, keepdims=True), jnp.max(s_page, axis=1, keepdims=True))
    e_local = jnp.exp(s_local - peak)
    e_page = jnp.exp(s_page - peak)
    norm = jnp.sum(e_local, axis=1, keepdims=True) + jnp.sum(e_page, axis=1, keepdims=True)
    p_local = (e_local / norm).astype(jnp.bfloat16)
    p_page = (e_page / norm).astype(jnp.bfloat16)
    paged = jnp.dot(p_page, wide, preferred_element_type=jnp.float32)
    for r in range(requests):
        at = slice(r * heads, (r + 1) * heads)
        out = jnp.dot(p_local[at], local_ref[r][:, :value], preferred_element_type=jnp.float32)
        out_ref[r] = (out + paged[at]).astype(jnp.bfloat16)


def tile_of(size, want):
    tile = min(size, want)
    while size % tile:
        tile -= LANES
    return tile


def per_device(
    hidden, norm_gain, routes, gate_weights, w_gate, w_up, w_down,
    queries, local_cache, cache_lengths, swap_pool, page_ids, page_owner,
):
    role_size, dev_size = lax.axis_size("role"), lax.axis_size("dev")
    devices = role_size * dev_size
    slices = devices // EXPERTS
    me = lax.axis_index("role") * dev_size + lax.axis_index("dev")
    me_arr = jnp.reshape(me, (1,)).astype(jnp.int32)
    rows, width = hidden.shape
    units = w_gate.shape[1]
    id_cols = pl.cdiv(devices, LANES) * LANES
    packed_width = width + LANES + id_cols
    half = dev_size * rows
    total_rows = role_size * half
    tk, tn = tile_of(width, 1024), tile_of(width, 512)
    weight_bytes = 2 * width * units
    groups = bit_groups(dev_size)
    weights_in = [pltpu.with_memory_space_constraint(w, pltpu.HBM) for w in (w_gate, w_up, w_down)]
    pool_in = pltpu.with_memory_space_constraint(swap_pool, pltpu.HBM)
    small_in = [
        pltpu.with_memory_space_constraint(a, pltpu.HBM)
        for a in (hidden, norm_gain, routes, gate_weights, page_ids)
    ]

    held = pl.pallas_call(
        pack_kernel,
        out_shape=jax.ShapeDtypeStruct((rows, packed_width), jnp.bfloat16),
        in_specs=[SM] + [HBM] * 5,
        out_specs=VM,
        scratch_shapes=[
            pltpu.VMEM(hidden.shape, hidden.dtype),
            pltpu.VMEM(norm_gain.shape, norm_gain.dtype),
            pltpu.VMEM(routes.shape, routes.dtype),
            pltpu.VMEM(gate_weights.shape, gate_weights.dtype),
            pltpu.VMEM(page_ids.shape, page_ids.dtype),
            pltpu.SemaphoreType.DMA((5,)),
        ],
        compiler_params=pltpu.CompilerParams(vmem_limit_bytes=6 << 20),
    )(me_arr, *small_in)

    def load(index, start):
        size = LOADS[index] * tk
        return pl.pallas_call(
            functools.partial(load_kernel, start=start),
            out_shape=pltpu.VMEM((size, units), jnp.bfloat16),
            in_specs=[HBM],
            out_specs=VM,
            scratch_shapes=[pltpu.SemaphoreType.DMA((2 * LOADS[index],))],
            compiler_params=pltpu.CompilerParams(vmem_limit_bytes=1 << 20),
            cost_estimate=pl.CostEstimate(flops=0, bytes_accessed=2 * size * units, transcendentals=0),
        )(weights_in[0])

    def swap(value, offset):
        return lax.ppermute(value, "dev", [(i, i ^ offset) for i in range(dev_size)])

    loaded = []
    taken = 0
    for k, (low, members) in enumerate(groups):
        got = [swap(held, offset << low) for offset in range(1, members)]
        if k < len(LOADS):
            loaded.append(load(k, taken))
            taken += LOADS[k] * tk
        held = pl.pallas_call(
            functools.partial(merge_kernel, low=low),
            out_shape=jax.ShapeDtypeStruct((members * held.shape[0], packed_width), jnp.bfloat16),
            in_specs=[SM] + [VM] * members,
            out_specs=VM,
            compiler_params=pltpu.CompilerParams(vmem_limit_bytes=6 << 20),
        )(me_arr, held, *got)
    other = role_swap(held)

    low, members = groups[-1]
    parts = role_size * members
    size = half // members
    own, *rest = pl.pallas_call(
        functools.partial(
            expert_kernel, tk=tk, tn=tn, base=width + LANES, rows=rows, slices=slices,
            groups=groups, loads=len(loaded), parts=parts,
        ),
        out_shape=[jax.ShapeDtypeStruct((size, width), jnp.float32)]
        + [jax.ShapeDtypeStruct((size, width), jnp.bfloat16)] * (parts - 1)
        + [jax.ShapeDtypeStruct((dev_size,) + swap_pool.shape[1:], jnp.bfloat16)] * 2,
        in_specs=[SM, VM, VM] + [VM] * len(loaded) + [HBM] * 4,
        out_specs=[VM] * (parts + 2),
        scratch_shapes=[
            pltpu.VMEM((GATE_SLOTS, tk, units), jnp.bfloat16),
            pltpu.VMEM((UP_SLOTS, tk, units), jnp.bfloat16),
            pltpu.VMEM((DOWN_SLOTS, units, tn), jnp.bfloat16),
            pltpu.VMEM((total_rows, units), jnp.float32),
            pltpu.VMEM((total_rows, units), jnp.float32),
            pltpu.VMEM((total_rows, units), jnp.bfloat16),
            pltpu.VMEM((total_rows, 1), jnp.float32),
            pltpu.VMEM((total_rows, id_cols), jnp.int32),
            pltpu.SMEM((total_rows, id_cols), jnp.int32),
            pltpu.SemaphoreType.DMA((GATE_SLOTS,)),
            pltpu.SemaphoreType.DMA((UP_SLOTS,)),
            pltpu.SemaphoreType.DMA((DOWN_SLOTS,)),
            pltpu.SemaphoreType.DMA,
            pltpu.SemaphoreType.DMA((2,)),
        ],
        compiler_params=pltpu.CompilerParams(vmem_limit_bytes=36 << 20),
        cost_estimate=pl.CostEstimate(
            flops=6 * total_rows * width * units, bytes_accessed=3 * weight_bytes, transcendentals=0
        ),
    )(me_arr, held, other, *loaded, *weights_in, pool_in)

    sends, near, far = rest[:-2], rest[-2], rest[-1]
    far = role_swap(far)
    got = []
    for n, value in enumerate(sends):
        flat = ((n + 1) // members) * dev_size + (((n + 1) % members) << low)
        got.append(lax.ppermute(value, ("role", "dev"), [(i, i ^ flat) for i in range(devices)]))
    page_shape = (dev_size, swap_pool.shape[1], 2 * swap_pool.shape[2])
    outgoing = pl.pallas_call(
        stack_kernel,
        out_shape=jax.ShapeDtypeStruct(page_shape, jnp.bfloat16),
        in_specs=[VM, VM],
        out_specs=VM,
        compiler_params=pltpu.CompilerParams(vmem_limit_bytes=8 << 20),
    )(near, far)
    arrived = lax.all_to_all(outgoing, "dev", split_axis=0, concat_axis=0, tiled=True)
    for low, members in reversed(groups[:-1]):
        count = own.shape[0] // members
        own, *sends = pl.pallas_call(
            functools.partial(fold_kernel, low=low, members=members, arrived=len(got)),
            out_shape=[jax.ShapeDtypeStruct((count, width), jnp.float32)]
            + [jax.ShapeDtypeStruct((count, width), jnp.bfloat16)] * (members - 1),
            in_specs=[SM] + [VM] * (1 + len(got)),
            out_specs=[VM] * members,
            compiler_params=pltpu.CompilerParams(vmem_limit_bytes=16 << 20),
        )(me_arr, own, *got)
        got = [swap(value, (n + 1) << low) for n, value in enumerate(sends)]
    query_rows = queries.shape[0] * queries.shape[1]
    bias, scores = pl.pallas_call(
        early_kernel,
        out_shape=(
            jax.ShapeDtypeStruct((query_rows, devices * swap_pool.shape[1]), jnp.float32),
            jax.ShapeDtypeStruct((query_rows, local_cache.shape[1]), jnp.float32),
        ),
        in_specs=[SM] * 2 + [VM] * 3,
        out_specs=(VM, VM),
        compiler_params=pltpu.CompilerParams(vmem_limit_bytes=16 << 20),
    )(me_arr, cache_lengths, page_owner, queries, local_cache)
    operands = (bias, scores, queries, local_cache, arrived, hidden, own, *got)
    attn_out, moe_out = pl.pallas_call(
        finish_kernel,
        out_shape=(
            jax.ShapeDtypeStruct(queries.shape[:2] + (queries.shape[2] - ROPE,), jnp.bfloat16),
            jax.ShapeDtypeStruct(hidden.shape, jnp.bfloat16),
        ),
        in_specs=[VM] * len(operands),
        out_specs=(VM, VM),
        compiler_params=pltpu.CompilerParams(vmem_limit_bytes=24 << 20),
    )(*operands)
    return (attn_out, moe_out)


def solution(mesh):
    in_specs = (
        P(("group", "role", "dev"), None),
        P(),
        P(("group", "role", "dev"), None),
        P(("group", "role", "dev"), None),
        P(None, ("role", "dev")),
        P(None, ("role", "dev")),
        P(("role", "dev"), None),
        P(("group", "role", "dev"), None, None),
        P(("group", "role", "dev"), None, None),
        P(("group", "role", "dev")),
        P(("group", "role", "dev"), None, None),
        P(("group", "role", "dev"), None),
        P(("group", "role", "dev"), None),
    )
    out_specs = (P(("group", "role", "dev"), None, None), P(("group", "role", "dev"), None))
    return jax.shard_map(per_device, mesh=mesh, in_specs=in_specs, out_specs=out_specs, check_vma=False)
```

```python
import functools

import jax
import jax.numpy as jnp
from jax import lax
from jax.experimental import pallas as pl
from jax.experimental.pallas import tpu as pltpu
from jax.sharding import PartitionSpec as P


ROPE = 64
EXPERTS = 16
LANES = 128

LOADS = (2, 2)
LEAD = 2
GATE_SLOTS = 2
UP_SLOTS = 3
DOWN_SLOTS = 6

score_scale = 192.0 ** (-0.5)
norm_eps = 1e-06


VM = pl.BlockSpec(memory_space=pltpu.VMEM)
SM = pl.BlockSpec(memory_space=pltpu.SMEM)
HBM = pl.BlockSpec(memory_space=pltpu.HBM)


def role_swap(x):
    size = lax.axis_size("role")
    return lax.ppermute(x, "role", [(i, size - 1 - i) for i in range(size)])


def pack_kernel(me_ref, hid_ref, gain_ref, routes_ref, weights_ref, ids_ref, out_ref, hid, gain, routes_v, weights_v, ids_v, sems):
    rows, width = hid.shape
    copies = [
        pltpu.make_async_copy(src, dst, sems.at[i])
        for i, (src, dst) in enumerate(
            ((hid_ref, hid), (gain_ref, gain), (routes_ref, routes_v), (weights_ref, weights_v), (ids_ref, ids_v))
        )
    ]
    for c in copies:
        c.start()
    for c in copies:
        c.wait()
    x = hid[...].astype(jnp.float32)
    inv = lax.rsqrt(jnp.mean(x * x, axis=1, keepdims=True) + norm_eps)
    gains = gain[...].astype(jnp.float32).reshape(1, width)
    normed = (x * inv * gains).astype(jnp.bfloat16)
    lane = lax.broadcasted_iota(jnp.int32, (rows, LANES), 1)
    expert = lax.rem(lane, EXPERTS)
    routes = routes_v[...]
    weights = weights_v[...]
    weight = jnp.zeros((rows, LANES), jnp.float32)
    for k in range(routes.shape[1]):
        weight = weight + jnp.where(routes[:, k : k + 1] == expert, weights[:, k : k + 1], 0.0)
    high = weight.astype(jnp.bfloat16).astype(jnp.float32)
    tail = jnp.where(lane < EXPERTS, high, jnp.where(lane < 2 * EXPERTS, weight - high, 0.0))
    tail = tail.astype(jnp.bfloat16)
    count = ids_v.shape[1]
    ids = jnp.broadcast_to(ids_v[...].astype(jnp.float32), (rows, count)).astype(jnp.bfloat16)
    out_ref[:, :width] = normed
    out_ref[:, width : width + LANES] = tail
    out_ref[:, width + LANES :] = jnp.zeros((rows, out_ref.shape[1] - width - LANES), jnp.bfloat16)
    out_ref[:, width + LANES : width + LANES + count] = ids


def bit_groups(size):
    groups = []
    top = size.bit_length() - 1
    while top > 0:
        length = min(2, top)
        top -= length
        groups.append((top, 1 << length))
    return groups


def block_of(index, groups):
    block = 0
    for low, members in reversed(groups):
        block = block * members + ((index >> low) & (members - 1))
    return block


def merge_kernel(me_ref, *refs, low):
    members = len(refs) - 1
    out_ref = refs[-1]
    rows = refs[0].shape[0]
    mine = (me_ref[0] >> low) & (members - 1)
    for place in range(members):

        @pl.when(mine == place)
        def _(place=place):
            for offset in range(members):
                at = (place ^ offset) * rows
                out_ref[at : at + rows] = refs[offset][...]


def load_kernel(src_ref, out_ref, sems, *, start):
    parts = sems.shape[0]
    step = out_ref.shape[0] // parts
    copies = [
        pltpu.make_async_copy(src_ref.at[pl.ds(start + i * step, step)], out_ref.at[pl.ds(i * step, step)], sems.at[i])
        for i in range(parts)
    ]
    for c in copies:
        c.start()
    for c in copies:
        c.wait()


def rows_of(xa_ref, xb_ref, i, tk):
    at = pl.ds(pl.multiple_of(i * tk, tk), tk)
    return jnp.concatenate([xa_ref[:, at], xb_ref[:, at]], axis=0)


def expert_kernel(*refs, tk, tn, base, rows, slices, groups, loads, parts):
    me_ref, xa_ref, xb_ref = refs[:3]
    pre_refs = refs[3 : 3 + loads]
    g_ref, u_ref, d_ref, pool_ref, keep_ref = refs[3 + loads : 8 + loads]
    send_refs = refs[8 + loads : 7 + loads + parts]
    near_ref, far_ref, gb, ub, db, ga, ua, h, wsel, vec, ids, semg, semu, semd, semi, semp = refs[7 + loads + parts :]
    width = d_ref.shape[1]
    n1, n2 = width // tk, width // tn
    ready = sum(r.shape[0] for r in pre_refs) // tk
    lead = min(LEAD, ready)
    nb, nd, ng = ub.shape[0], db.shape[0], gb.shape[0]
    half = xa_ref.shape[0]
    me = me_ref[0]

    def cg(i):
        s = lax.rem(i - ready, ng)
        return pltpu.make_async_copy(g_ref.at[pl.ds(i * tk, tk)], gb.at[s], semg.at[s])

    def cu(i):
        s = lax.rem(i, nb)
        return pltpu.make_async_copy(u_ref.at[pl.ds(i * tk, tk)], ub.at[s], semu.at[s])

    def cd(j):
        s = lax.rem(j, nd)
        cols = pl.ds(pl.multiple_of(j * tn, tn), tn)
        return pltpu.make_async_copy(d_ref.at[:, cols], db.at[s], semd.at[s])

    for i in range(min(nb, n1)):
        cu(i).start()
    for i in range(ready, min(ready + ng, n1)):
        cg(i).start()
    cols = vec.shape[1]
    vec[:half] = xa_ref[:, base : base + cols].astype(jnp.float32).astype(jnp.int32)
    vec[half:] = xb_ref[:, base : base + cols].astype(jnp.float32).astype(jnp.int32)
    move = pltpu.make_async_copy(vec, ids, semi)
    move.start()

    ga[...] = jnp.zeros_like(ga)
    ua[...] = jnp.zeros_like(ua)
    expert = me // slices
    lane = lax.broadcasted_iota(jnp.int32, (half, LANES), 1)
    chosen = (lane == expert) | (lane == expert + EXPERTS)
    for i, ref in enumerate((xa_ref, xb_ref)):
        tail = ref[:, width : width + LANES].astype(jnp.float32)
        wsel[i * half : (i + 1) * half] = jnp.sum(jnp.where(chosen, tail, 0.0), axis=1, keepdims=True)

    peers = near_ref.shape[0]

    def page_start(d):
        row = block_of(d, groups) * rows
        for n, ref in enumerate((near_ref, far_ref)):
            page = pool_ref.at[ids[row + n * half, me]]
            pltpu.make_async_copy(page, ref.at[d], semp.at[n]).start()

    def gate(i, weights):
        ga[...] += jnp.dot(rows_of(xa_ref, xb_ref, i, tk), weights, preferred_element_type=jnp.float32)

    def up(i):
        cu(i).wait()
        xs = rows_of(xa_ref, xb_ref, i, tk)
        ua[...] += jnp.dot(xs, ub[lax.rem(i, nb)], preferred_element_type=jnp.float32)

        @pl.when(i + nb < n1)
        def _():
            cu(i + nb).start()

        @pl.when((i + nd >= n1) & (i + nd - n1 < n2))
        def _():
            cd(i + nd - n1).start()

    for j in range(min(n2, max(0, nd - n1))):
        cd(j).start()
    step = 0
    for ref in pre_refs:
        for k in range(ref.shape[0] // tk):
            gate(step, ref[k * tk : (k + 1) * tk, :])
            if step == 0:
                move.wait()
                for d in range(peers):
                    page_start(d)
            if step >= lead:
                up(step - lead)
            step += 1

    def late(i, c):
        cg(i).wait()
        gate(i, gb[lax.rem(i - ready, ng)])

        @pl.when(i + ng < n1)
        def _():
            cg(i + ng).start()

        up(i - lead)
        return c

    def rest(i, c):
        up(i)
        return c

    lax.fori_loop(ready, n1, late, 0)
    lax.fori_loop(n1 - lead, n1, rest, 0)
    g = ga[...]
    h[...] = ((g / (1.0 + jnp.exp(-g))) * ua[...]).astype(jnp.bfloat16)

    low, members = groups[-1]
    place = (me >> low) & (members - 1)
    size = half // members

    def down(j, c):
        cd(j).wait()
        at = pl.ds(pl.multiple_of(j * tn, tn), tn)
        out = jnp.dot(h[...], db[lax.rem(j, nd)], preferred_element_type=jnp.float32)
        out = out * wsel[...]
        for n, ref in enumerate((keep_ref,) + tuple(send_refs)):
            start = (n // members) * half
            want = place ^ (n % members)
            block = out[start : start + size]
            for p in range(1, members):
                block = jnp.where(want == p, out[start + p * size : start + (p + 1) * size], block)
            ref[:, at] = block.astype(ref.dtype)

        @pl.when(j + nd < n2)
        def _():
            cd(j + nd).start()

        return c

    lax.fori_loop(0, n2, down, 0, unroll=2)
    for n, ref in enumerate((near_ref, far_ref)):
        pltpu.make_async_copy(ref, ref, semp.at[n]).wait()


def fold_kernel(me_ref, *refs, low, members, arrived):
    own_ref, got_refs = refs[0], refs[1 : 1 + arrived]
    keep_ref, send_refs = refs[1 + arrived], refs[2 + arrived :]
    rows = keep_ref.shape[0]
    mine = (me_ref[0] >> low) & (members - 1)

    def block(place):
        at = slice(place * rows, (place + 1) * rows)
        total = own_ref[at]
        for ref in got_refs:
            total = total + ref[at].astype(jnp.float32)
        return total

    for place in range(members):

        @pl.when(mine == place)
        def _(place=place):
            for offset in range(1, members):
                send_refs[offset - 1][...] = block(place ^ offset).astype(jnp.bfloat16)
            keep_ref[...] = block(place)


def stack_kernel(near_ref, far_ref, out_ref):
    width = near_ref.shape[2]
    value = width - ROPE
    for n, ref in enumerate((near_ref, far_ref)):
        out_ref[:, :, n * value : (n + 1) * value] = ref[:, :, :value]
        out_ref[:, :, 2 * value + n * ROPE : 2 * value + (n + 1) * ROPE] = ref[:, :, value:]


def early_kernel(me_ref, len_ref, owner_ref, q_ref, local_ref, bias_ref, peak_ref, sum_ref, part_ref):
    requests, heads, _ = q_ref.shape
    local_len = local_ref.shape[1]
    devices = owner_ref.shape[1]
    keys = bias_ref.shape[1]
    page_len = keys // devices
    half = devices // 2
    mine = me_ref[0] // half
    holder = lax.broadcasted_iota(jnp.int32, (devices, keys), 0)
    slot = lax.broadcasted_iota(jnp.int32, (devices, keys), 1) // page_len
    sender = jnp.where(mine == 0, slot, jnp.where(slot < half, slot + half, slot - half))
    owner = jnp.broadcast_to(jnp.transpose(owner_ref[...].astype(jnp.float32)), holder.shape)
    key_owner = jnp.sum(jnp.where(holder == sender, owner, 0.0), axis=0, keepdims=True)
    request = (lax.broadcasted_iota(jnp.int32, bias_ref.shape, 0) // heads).astype(jnp.float32)
    bias_ref[...] = jnp.where(key_owner == request, 0.0, -jnp.inf)
    pos = lax.broadcasted_iota(jnp.int32, (heads, local_len), 1)
    nt = (((1,), (1,)), ((), ()))
    for r in range(requests):
        s = lax.dot_general(q_ref[r], local_ref[r], nt, preferred_element_type=jnp.float32) * score_scale
        s = jnp.where(pos < len_ref[r], s, -jnp.inf)
        at = slice(r * heads, (r + 1) * heads)
        peak = jnp.max(s, axis=1, keepdims=True)
        e = jnp.exp(s - peak)
        peak_ref[at] = peak
        sum_ref[at] = jnp.sum(e, axis=1, keepdims=True)
        local = local_ref[r][:, : part_ref.shape[1]]
        part_ref[at] = jnp.dot(e.astype(jnp.bfloat16), local, preferred_element_type=jnp.float32)


def finish_kernel(bias_ref, peak_ref, sum_ref, part_ref, q_ref, page_ref, hid_ref, own_ref, *refs):
    got_refs, out_ref, moe_ref = refs[:-2], refs[-2], refs[-1]
    total = own_ref[...]
    for ref in got_refs:
        total = total + ref[...].astype(jnp.float32)
    moe_ref[...] = (hid_ref[...].astype(jnp.float32) + total).astype(jnp.bfloat16)

    requests, heads, width = q_ref.shape
    value = out_ref.shape[2]
    peers, page_len, _ = page_ref.shape

    def keys_of(start, size):
        part = page_ref[:, :, start : start + size]
        return part.reshape(peers * page_len, size)

    wide = jnp.concatenate([keys_of(0, value), keys_of(value, value)], axis=0)
    thin = jnp.concatenate([keys_of(2 * value, ROPE), keys_of(2 * value + ROPE, ROPE)], axis=0)
    nt = (((1,), (1,)), ((), ()))
    queries = q_ref[...].reshape(requests * heads, width)
    s_page = lax.dot_general(queries[:, :value], wide, nt, preferred_element_type=jnp.float32)
    s_page = s_page + lax.dot_general(queries[:, value:], thin, nt, preferred_element_type=jnp.float32)
    s_page = s_page * score_scale + bias_ref[...]
    peak = jnp.maximum(peak_ref[...], jnp.max(s_page, axis=1, keepdims=True))
    scale = jnp.exp(peak_ref[...] - peak)
    e_page = jnp.exp(s_page - peak)
    norm = sum_ref[...] * scale + jnp.sum(e_page, axis=1, keepdims=True)
    p_page = (e_page / norm).astype(jnp.bfloat16)
    out = jnp.dot(p_page, wide, preferred_element_type=jnp.float32) + part_ref[...] * (scale / norm)
    for r in range(requests):
        out_ref[r] = out[r * heads : (r + 1) * heads].astype(jnp.bfloat16)


def tile_of(size, want):
    tile = min(size, want)
    while size % tile:
        tile -= LANES
    return tile


def per_device(
    hidden, norm_gain, routes, gate_weights, w_gate, w_up, w_down,
    queries, local_cache, cache_lengths, swap_pool, page_ids, page_owner,
):
    role_size, dev_size = lax.axis_size("role"), lax.axis_size("dev")
    devices = role_size * dev_size
    slices = devices // EXPERTS
    me = lax.axis_index("role") * dev_size + lax.axis_index("dev")
    me_arr = jnp.reshape(me, (1,)).astype(jnp.int32)
    rows, width = hidden.shape
    units = w_gate.shape[1]
    id_cols = pl.cdiv(devices, LANES) * LANES
    packed_width = width + LANES + id_cols
    half = dev_size * rows
    total_rows = role_size * half
    tk, tn = tile_of(width, 1024), tile_of(width, 512)
    weight_bytes = 2 * width * units
    groups = bit_groups(dev_size)
    weights_in = [pltpu.with_memory_space_constraint(w, pltpu.HBM) for w in (w_gate, w_up, w_down)]
    pool_in = pltpu.with_memory_space_constraint(swap_pool, pltpu.HBM)
    small_in = [
        pltpu.with_memory_space_constraint(a, pltpu.HBM)
        for a in (hidden, norm_gain, routes, gate_weights, page_ids)
    ]

    held = pl.pallas_call(
        pack_kernel,
        out_shape=jax.ShapeDtypeStruct((rows, packed_width), jnp.bfloat16),
        in_specs=[SM] + [HBM] * 5,
        out_specs=VM,
        scratch_shapes=[
            pltpu.VMEM(hidden.shape, hidden.dtype),
            pltpu.VMEM(norm_gain.shape, norm_gain.dtype),
            pltpu.VMEM(routes.shape, routes.dtype),
            pltpu.VMEM(gate_weights.shape, gate_weights.dtype),
            pltpu.VMEM(page_ids.shape, page_ids.dtype),
            pltpu.SemaphoreType.DMA((5,)),
        ],
        compiler_params=pltpu.CompilerParams(vmem_limit_bytes=6 << 20),
    )(me_arr, *small_in)

    def load(index, start):
        size = LOADS[index] * tk
        return pl.pallas_call(
            functools.partial(load_kernel, start=start),
            out_shape=pltpu.VMEM((size, units), jnp.bfloat16),
            in_specs=[HBM],
            out_specs=VM,
            scratch_shapes=[pltpu.SemaphoreType.DMA((2 * LOADS[index],))],
            compiler_params=pltpu.CompilerParams(vmem_limit_bytes=1 << 20),
            cost_estimate=pl.CostEstimate(flops=0, bytes_accessed=2 * size * units, transcendentals=0),
        )(weights_in[0])

    def swap(value, offset):
        return lax.ppermute(value, "dev", [(i, i ^ offset) for i in range(dev_size)])

    loaded = []
    taken = 0
    for k, (low, members) in enumerate(groups):
        got = [swap(held, offset << low) for offset in range(1, members)]
        if k < len(LOADS):
            loaded.append(load(k, taken))
            taken += LOADS[k] * tk
        held = pl.pallas_call(
            functools.partial(merge_kernel, low=low),
            out_shape=jax.ShapeDtypeStruct((members * held.shape[0], packed_width), jnp.bfloat16),
            in_specs=[SM] + [VM] * members,
            out_specs=VM,
            compiler_params=pltpu.CompilerParams(vmem_limit_bytes=6 << 20),
        )(me_arr, held, *got)
    other = role_swap(held)

    low, members = groups[-1]
    parts = role_size * members
    size = half // members
    own, *rest = pl.pallas_call(
        functools.partial(
            expert_kernel, tk=tk, tn=tn, base=width + LANES, rows=rows, slices=slices,
            groups=groups, loads=len(loaded), parts=parts,
        ),
        out_shape=[jax.ShapeDtypeStruct((size, width), jnp.float32)]
        + [jax.ShapeDtypeStruct((size, width), jnp.bfloat16)] * (parts - 1)
        + [jax.ShapeDtypeStruct((dev_size,) + swap_pool.shape[1:], jnp.bfloat16)] * 2,
        in_specs=[SM, VM, VM] + [VM] * len(loaded) + [HBM] * 4,
        out_specs=[VM] * (parts + 2),
        scratch_shapes=[
            pltpu.VMEM((GATE_SLOTS, tk, units), jnp.bfloat16),
            pltpu.VMEM((UP_SLOTS, tk, units), jnp.bfloat16),
            pltpu.VMEM((DOWN_SLOTS, units, tn), jnp.bfloat16),
            pltpu.VMEM((total_rows, units), jnp.float32),
            pltpu.VMEM((total_rows, units), jnp.float32),
            pltpu.VMEM((total_rows, units), jnp.bfloat16),
            pltpu.VMEM((total_rows, 1), jnp.float32),
            pltpu.VMEM((total_rows, id_cols), jnp.int32),
            pltpu.SMEM((total_rows, id_cols), jnp.int32),
            pltpu.SemaphoreType.DMA((GATE_SLOTS,)),
            pltpu.SemaphoreType.DMA((UP_SLOTS,)),
            pltpu.SemaphoreType.DMA((DOWN_SLOTS,)),
            pltpu.SemaphoreType.DMA,
            pltpu.SemaphoreType.DMA((2,)),
        ],
        compiler_params=pltpu.CompilerParams(vmem_limit_bytes=36 << 20),
        cost_estimate=pl.CostEstimate(
            flops=6 * total_rows * width * units, bytes_accessed=3 * weight_bytes, transcendentals=0
        ),
    )(me_arr, held, other, *loaded, *weights_in, pool_in)

    sends, near, far = rest[:-2], rest[-2], rest[-1]
    far = role_swap(far)
    got = []
    for n, value in enumerate(sends):
        flat = ((n + 1) // members) * dev_size + (((n + 1) % members) << low)
        got.append(lax.ppermute(value, ("role", "dev"), [(i, i ^ flat) for i in range(devices)]))
    page_shape = (dev_size, swap_pool.shape[1], 2 * swap_pool.shape[2])
    outgoing = pl.pallas_call(
        stack_kernel,
        out_shape=jax.ShapeDtypeStruct(page_shape, jnp.bfloat16),
        in_specs=[VM, VM],
        out_specs=VM,
        compiler_params=pltpu.CompilerParams(vmem_limit_bytes=8 << 20),
    )(near, far)
    arrived = lax.all_to_all(outgoing, "dev", split_axis=0, concat_axis=0, tiled=True)
    for low, members in reversed(groups[:-1]):
        count = own.shape[0] // members
        own, *sends = pl.pallas_call(
            functools.partial(fold_kernel, low=low, members=members, arrived=len(got)),
            out_shape=[jax.ShapeDtypeStruct((count, width), jnp.float32)]
            + [jax.ShapeDtypeStruct((count, width), jnp.bfloat16)] * (members - 1),
            in_specs=[SM] + [VM] * (1 + len(got)),
            out_specs=[VM] * members,
            compiler_params=pltpu.CompilerParams(vmem_limit_bytes=16 << 20),
        )(me_arr, own, *got)
        got = [swap(value, (n + 1) << low) for n, value in enumerate(sends)]
    query_rows = queries.shape[0] * queries.shape[1]
    bias, peaks, sums, local_out = pl.pallas_call(
        early_kernel,
        out_shape=(
            jax.ShapeDtypeStruct((query_rows, devices * swap_pool.shape[1]), jnp.float32),
            jax.ShapeDtypeStruct((query_rows, 1), jnp.float32),
            jax.ShapeDtypeStruct((query_rows, 1), jnp.float32),
            jax.ShapeDtypeStruct((query_rows, queries.shape[2] - ROPE), jnp.float32),
        ),
        in_specs=[SM] * 2 + [VM] * 3,
        out_specs=(VM,) * 4,
        compiler_params=pltpu.CompilerParams(vmem_limit_bytes=16 << 20),
    )(me_arr, cache_lengths, page_owner, queries, local_cache)
    operands = (bias, peaks, sums, local_out, queries, arrived, hidden, own, *got)
    attn_out, moe_out = pl.pallas_call(
        finish_kernel,
        out_shape=(
            jax.ShapeDtypeStruct(queries.shape[:2] + (queries.shape[2] - ROPE,), jnp.bfloat16),
            jax.ShapeDtypeStruct(hidden.shape, jnp.bfloat16),
        ),
        in_specs=[VM] * len(operands),
        out_specs=(VM, VM),
        compiler_params=pltpu.CompilerParams(vmem_limit_bytes=24 << 20),
    )(*operands)
    return (attn_out, moe_out)


def solution(mesh):
    in_specs = (
        P(("group", "role", "dev"), None),
        P(),
        P(("group", "role", "dev"), None),
        P(("group", "role", "dev"), None),
        P(None, ("role", "dev")),
        P(None, ("role", "dev")),
        P(("role", "dev"), None),
        P(("group", "role", "dev"), None, None),
        P(("group", "role", "dev"), None, None),
        P(("group", "role", "dev")),
        P(("group", "role", "dev"), None, None),
        P(("group", "role", "dev"), None),
        P(("group", "role", "dev"), None),
    )
    out_specs = (P(("group", "role", "dev"), None, None), P(("group", "role", "dev"), None))
    return jax.shard_map(per_device, mesh=mesh, in_specs=in_specs, out_specs=out_specs, check_vma=False)
```

```python
import functools

import jax
import jax.numpy as jnp
from jax import lax
from jax.experimental import pallas as pl
from jax.experimental.pallas import tpu as pltpu
from jax.sharding import PartitionSpec as P


ROPE = 64
EXPERTS = 16
LANES = 128

LOADS = (2, 2)
LEAD = 2
GATE_SLOTS = 2
UP_SLOTS = 3
DOWN_SLOTS = 6

score_scale = 192.0 ** (-0.5)
norm_eps = 1e-06


VM = pl.BlockSpec(memory_space=pltpu.VMEM)
SM = pl.BlockSpec(memory_space=pltpu.SMEM)
HBM = pl.BlockSpec(memory_space=pltpu.HBM)


def role_swap(x):
    size = lax.axis_size("role")
    return lax.ppermute(x, "role", [(i, size - 1 - i) for i in range(size)])


def pack_kernel(me_ref, hid_ref, gain_ref, routes_ref, weights_ref, ids_ref, out_ref, hid, gain, routes_v, weights_v, ids_v, sems):
    rows, width = hid.shape
    copies = [
        pltpu.make_async_copy(src, dst, sems.at[i])
        for i, (src, dst) in enumerate(
            ((hid_ref, hid), (gain_ref, gain), (routes_ref, routes_v), (weights_ref, weights_v), (ids_ref, ids_v))
        )
    ]
    for c in copies:
        c.start()
    for c in copies:
        c.wait()
    x = hid[...].astype(jnp.float32)
    inv = lax.rsqrt(jnp.mean(x * x, axis=1, keepdims=True) + norm_eps)
    gains = gain[...].astype(jnp.float32).reshape(1, width)
    normed = (x * inv * gains).astype(jnp.bfloat16)
    lane = lax.broadcasted_iota(jnp.int32, (rows, LANES), 1)
    expert = lax.rem(lane, EXPERTS)
    routes = routes_v[...]
    weights = weights_v[...]
    weight = jnp.zeros((rows, LANES), jnp.float32)
    for k in range(routes.shape[1]):
        weight = weight + jnp.where(routes[:, k : k + 1] == expert, weights[:, k : k + 1], 0.0)
    high = weight.astype(jnp.bfloat16).astype(jnp.float32)
    tail = jnp.where(lane < EXPERTS, high, jnp.where(lane < 2 * EXPERTS, weight - high, 0.0))
    tail = tail.astype(jnp.bfloat16)
    count = ids_v.shape[1]
    ids = jnp.broadcast_to(ids_v[...].astype(jnp.float32), (rows, count)).astype(jnp.bfloat16)
    out_ref[:, :width] = normed
    out_ref[:, width : width + LANES] = tail
    out_ref[:, width + LANES :] = jnp.zeros((rows, out_ref.shape[1] - width - LANES), jnp.bfloat16)
    out_ref[:, width + LANES : width + LANES + count] = ids


def bit_groups(size):
    groups = []
    top = size.bit_length() - 1
    while top > 0:
        length = min(2, top)
        top -= length
        groups.append((top, 1 << length))
    return groups


def block_of(index, groups):
    block = 0
    for low, members in reversed(groups):
        block = block * members + ((index >> low) & (members - 1))
    return block


def merge_kernel(me_ref, *refs, low):
    members = len(refs) - 1
    out_ref = refs[-1]
    rows = refs[0].shape[0]
    mine = (me_ref[0] >> low) & (members - 1)
    for place in range(members):

        @pl.when(mine == place)
        def _(place=place):
            for offset in range(members):
                at = (place ^ offset) * rows
                out_ref[at : at + rows] = refs[offset][...]


def load_kernel(src_ref, out_ref, sems, *, start):
    parts = sems.shape[0]
    step = out_ref.shape[0] // parts
    copies = [
        pltpu.make_async_copy(src_ref.at[pl.ds(start + i * step, step)], out_ref.at[pl.ds(i * step, step)], sems.at[i])
        for i in range(parts)
    ]
    for c in copies:
        c.start()
    for c in copies:
        c.wait()


def rows_of(xa_ref, xb_ref, i, tk):
    at = pl.ds(pl.multiple_of(i * tk, tk), tk)
    return jnp.concatenate([xa_ref[:, at], xb_ref[:, at]], axis=0)


def expert_kernel(*refs, tk, tn, base, rows, slices, groups, loads, parts):
    me_ref, xa_ref, xb_ref = refs[:3]
    pre_refs = refs[3 : 3 + loads]
    g_ref, u_ref, d_ref, pool_ref, keep_ref = refs[3 + loads : 8 + loads]
    send_refs = refs[8 + loads : 7 + loads + parts]
    near_ref, far_ref, gb, ub, db, ga, ua, h, wsel, vec, ids, semg, semu, semd, semi, semp = refs[7 + loads + parts :]
    width = d_ref.shape[1]
    n1, n2 = width // tk, width // tn
    ready = sum(r.shape[0] for r in pre_refs) // tk
    lead = min(LEAD, ready)
    nb, nd, ng = ub.shape[0], db.shape[0], gb.shape[0]
    half = xa_ref.shape[0]
    me = me_ref[0]

    def cg(i):
        s = lax.rem(i - ready, ng)
        return pltpu.make_async_copy(g_ref.at[pl.ds(i * tk, tk)], gb.at[s], semg.at[s])

    def cu(i):
        s = lax.rem(i, nb)
        return pltpu.make_async_copy(u_ref.at[pl.ds(i * tk, tk)], ub.at[s], semu.at[s])

    def cd(j):
        s = lax.rem(j, nd)
        cols = pl.ds(pl.multiple_of(j * tn, tn), tn)
        return pltpu.make_async_copy(d_ref.at[:, cols], db.at[s], semd.at[s])

    for i in range(min(nb, n1)):
        cu(i).start()
    for i in range(ready, min(ready + ng, n1)):
        cg(i).start()
    cols = vec.shape[1]
    vec[:half] = xa_ref[:, base : base + cols].astype(jnp.float32).astype(jnp.int32)
    vec[half:] = xb_ref[:, base : base + cols].astype(jnp.float32).astype(jnp.int32)
    move = pltpu.make_async_copy(vec, ids, semi)
    move.start()

    ga[...] = jnp.zeros_like(ga)
    ua[...] = jnp.zeros_like(ua)
    expert = me // slices
    lane = lax.broadcasted_iota(jnp.int32, (half, LANES), 1)
    chosen = (lane == expert) | (lane == expert + EXPERTS)
    for i, ref in enumerate((xa_ref, xb_ref)):
        tail = ref[:, width : width + LANES].astype(jnp.float32)
        wsel[i * half : (i + 1) * half] = jnp.sum(jnp.where(chosen, tail, 0.0), axis=1, keepdims=True)

    peers = near_ref.shape[0]

    def page_start(d):
        row = block_of(d, groups) * rows
        for n, ref in enumerate((near_ref, far_ref)):
            page = pool_ref.at[ids[row + n * half, me]]
            pltpu.make_async_copy(page, ref.at[d], semp.at[n]).start()

    def gate(i, weights):
        ga[...] += jnp.dot(rows_of(xa_ref, xb_ref, i, tk), weights, preferred_element_type=jnp.float32)

    def up(i):
        cu(i).wait()
        xs = rows_of(xa_ref, xb_ref, i, tk)
        ua[...] += jnp.dot(xs, ub[lax.rem(i, nb)], preferred_element_type=jnp.float32)

        @pl.when(i + nb < n1)
        def _():
            cu(i + nb).start()

        @pl.when((i + nd >= n1) & (i + nd - n1 < n2))
        def _():
            cd(i + nd - n1).start()

    for j in range(min(n2, max(0, nd - n1))):
        cd(j).start()
    step = 0
    for ref in pre_refs:
        for k in range(ref.shape[0] // tk):
            gate(step, ref[k * tk : (k + 1) * tk, :])
            if step == 0:
                move.wait()
                for d in range(peers):
                    page_start(d)
            if step >= lead:
                up(step - lead)
            step += 1

    def late(i, c):
        cg(i).wait()
        gate(i, gb[lax.rem(i - ready, ng)])

        @pl.when(i + ng < n1)
        def _():
            cg(i + ng).start()

        up(i - lead)
        return c

    def rest(i, c):
        up(i)
        return c

    lax.fori_loop(ready, n1, late, 0)
    lax.fori_loop(n1 - lead, n1, rest, 0)
    g = ga[...]
    h[...] = ((g / (1.0 + jnp.exp(-g))) * ua[...]).astype(jnp.bfloat16)

    low, members = groups[-1]
    place = (me >> low) & (members - 1)
    size = half // members

    def down(j, c):
        cd(j).wait()
        at = pl.ds(pl.multiple_of(j * tn, tn), tn)
        out = jnp.dot(h[...], db[lax.rem(j, nd)], preferred_element_type=jnp.float32)
        out = out * wsel[...]
        for n, ref in enumerate((keep_ref,) + tuple(send_refs)):
            start = (n // members) * half
            want = place ^ (n % members)
            block = out[start : start + size]
            for p in range(1, members):
                block = jnp.where(want == p, out[start + p * size : start + (p + 1) * size], block)
            ref[:, at] = block.astype(ref.dtype)

        @pl.when(j + nd < n2)
        def _():
            cd(j + nd).start()

        return c

    lax.fori_loop(0, n2, down, 0, unroll=2)
    for n, ref in enumerate((near_ref, far_ref)):
        pltpu.make_async_copy(ref, ref, semp.at[n]).wait()


def fold_kernel(me_ref, *refs, low, members, arrived):
    own_ref, got_refs = refs[0], refs[1 : 1 + arrived]
    keep_ref, send_refs = refs[1 + arrived], refs[2 + arrived :]
    rows = keep_ref.shape[0]
    mine = (me_ref[0] >> low) & (members - 1)

    def block(place):
        at = slice(place * rows, (place + 1) * rows)
        total = own_ref[at]
        for ref in got_refs:
            total = total + ref[at].astype(jnp.float32)
        return total

    for place in range(members):

        @pl.when(mine == place)
        def _(place=place):
            for offset in range(1, members):
                send_refs[offset - 1][...] = block(place ^ offset).astype(jnp.bfloat16)
            keep_ref[...] = block(place)


def stack_kernel(near_ref, far_ref, out_ref, thin, sems):
    value = near_ref.shape[2] - ROPE
    copies = []
    for n, ref in enumerate((near_ref, far_ref)):
        target = out_ref.at[:, :, n * value : (n + 1) * value]
        copies.append(pltpu.make_async_copy(ref.at[:, :, :value], target, sems.at[n]))
        copies[-1].start()
    for n, ref in enumerate((near_ref, far_ref)):
        thin[:, :, n * ROPE : (n + 1) * ROPE] = ref[:, :, value:]
    copies.append(pltpu.make_async_copy(thin, out_ref.at[:, :, 2 * value :], sems.at[2]))
    copies[-1].start()
    for c in copies:
        c.wait()


def early_kernel(me_ref, len_ref, owner_ref, q_ref, local_ref, bias_ref, peak_ref, sum_ref, part_ref):
    requests, heads, _ = q_ref.shape
    local_len = local_ref.shape[1]
    devices = owner_ref.shape[1]
    keys = bias_ref.shape[1]
    page_len = keys // devices
    half = devices // 2
    mine = me_ref[0] // half
    holder = lax.broadcasted_iota(jnp.int32, (devices, keys), 0)
    slot = lax.broadcasted_iota(jnp.int32, (devices, keys), 1) // page_len
    sender = jnp.where(mine == 0, slot, jnp.where(slot < half, slot + half, slot - half))
    owner = jnp.broadcast_to(jnp.transpose(owner_ref[...].astype(jnp.float32)), holder.shape)
    key_owner = jnp.sum(jnp.where(holder == sender, owner, 0.0), axis=0, keepdims=True)
    request = (lax.broadcasted_iota(jnp.int32, bias_ref.shape, 0) // heads).astype(jnp.float32)
    bias_ref[...] = jnp.where(key_owner == request, 0.0, -jnp.inf)
    pos = lax.broadcasted_iota(jnp.int32, (heads, local_len), 1)
    nt = (((1,), (1,)), ((), ()))
    for r in range(requests):
        s = lax.dot_general(q_ref[r], local_ref[r], nt, preferred_element_type=jnp.float32) * score_scale
        s = jnp.where(pos < len_ref[r], s, -jnp.inf)
        at = slice(r * heads, (r + 1) * heads)
        peak = jnp.max(s, axis=1, keepdims=True)
        e = jnp.exp(s - peak)
        peak_ref[at] = peak
        sum_ref[at] = jnp.sum(e, axis=1, keepdims=True)
        local = local_ref[r][:, : part_ref.shape[1]]
        part_ref[at] = jnp.dot(e.astype(jnp.bfloat16), local, preferred_element_type=jnp.float32)


def finish_kernel(bias_ref, peak_ref, sum_ref, part_ref, q_ref, page_ref, hid_ref, own_ref, *refs):
    got_refs, out_ref, moe_ref = refs[:-2], refs[-2], refs[-1]
    total = own_ref[...]
    for ref in got_refs:
        total = total + ref[...].astype(jnp.float32)
    moe_ref[...] = (hid_ref[...].astype(jnp.float32) + total).astype(jnp.bfloat16)

    requests, heads, width = q_ref.shape
    value = out_ref.shape[2]
    peers, page_len, _ = page_ref.shape

    def keys_of(start, size):
        part = page_ref[:, :, start : start + size]
        return part.reshape(peers * page_len, size)

    wide = jnp.concatenate([keys_of(0, value), keys_of(value, value)], axis=0)
    thin = jnp.concatenate([keys_of(2 * value, ROPE), keys_of(2 * value + ROPE, ROPE)], axis=0)
    nt = (((1,), (1,)), ((), ()))
    queries = q_ref[...].reshape(requests * heads, width)
    s_page = lax.dot_general(queries[:, :value], wide, nt, preferred_element_type=jnp.float32)
    s_page = s_page + lax.dot_general(queries[:, value:], thin, nt, preferred_element_type=jnp.float32)
    s_page = s_page * score_scale + bias_ref[...]
    peak = jnp.maximum(peak_ref[...], jnp.max(s_page, axis=1, keepdims=True))
    scale = jnp.exp(peak_ref[...] - peak)
    e_page = jnp.exp(s_page - peak)
    norm = sum_ref[...] * scale + jnp.sum(e_page, axis=1, keepdims=True)
    p_page = (e_page / norm).astype(jnp.bfloat16)
    out = jnp.dot(p_page, wide, preferred_element_type=jnp.float32) + part_ref[...] * (scale / norm)
    for r in range(requests):
        out_ref[r] = out[r * heads : (r + 1) * heads].astype(jnp.bfloat16)


def tile_of(size, want):
    tile = min(size, want)
    while size % tile:
        tile -= LANES
    return tile


def per_device(
    hidden, norm_gain, routes, gate_weights, w_gate, w_up, w_down,
    queries, local_cache, cache_lengths, swap_pool, page_ids, page_owner,
):
    role_size, dev_size = lax.axis_size("role"), lax.axis_size("dev")
    devices = role_size * dev_size
    slices = devices // EXPERTS
    me = lax.axis_index("role") * dev_size + lax.axis_index("dev")
    me_arr = jnp.reshape(me, (1,)).astype(jnp.int32)
    rows, width = hidden.shape
    units = w_gate.shape[1]
    id_cols = pl.cdiv(devices, LANES) * LANES
    packed_width = width + LANES + id_cols
    half = dev_size * rows
    total_rows = role_size * half
    tk, tn = tile_of(width, 1024), tile_of(width, 512)
    weight_bytes = 2 * width * units
    groups = bit_groups(dev_size)
    weights_in = [pltpu.with_memory_space_constraint(w, pltpu.HBM) for w in (w_gate, w_up, w_down)]
    pool_in = pltpu.with_memory_space_constraint(swap_pool, pltpu.HBM)
    small_in = [
        pltpu.with_memory_space_constraint(a, pltpu.HBM)
        for a in (hidden, norm_gain, routes, gate_weights, page_ids)
    ]

    held = pl.pallas_call(
        pack_kernel,
        out_shape=jax.ShapeDtypeStruct((rows, packed_width), jnp.bfloat16),
        in_specs=[SM] + [HBM] * 5,
        out_specs=VM,
        scratch_shapes=[
            pltpu.VMEM(hidden.shape, hidden.dtype),
            pltpu.VMEM(norm_gain.shape, norm_gain.dtype),
            pltpu.VMEM(routes.shape, routes.dtype),
            pltpu.VMEM(gate_weights.shape, gate_weights.dtype),
            pltpu.VMEM(page_ids.shape, page_ids.dtype),
            pltpu.SemaphoreType.DMA((5,)),
        ],
        compiler_params=pltpu.CompilerParams(vmem_limit_bytes=6 << 20),
    )(me_arr, *small_in)

    def load(index, start):
        size = LOADS[index] * tk
        return pl.pallas_call(
            functools.partial(load_kernel, start=start),
            out_shape=pltpu.VMEM((size, units), jnp.bfloat16),
            in_specs=[HBM],
            out_specs=VM,
            scratch_shapes=[pltpu.SemaphoreType.DMA((2 * LOADS[index],))],
            compiler_params=pltpu.CompilerParams(vmem_limit_bytes=1 << 20),
            cost_estimate=pl.CostEstimate(flops=0, bytes_accessed=2 * size * units, transcendentals=0),
        )(weights_in[0])

    def swap(value, offset):
        return lax.ppermute(value, "dev", [(i, i ^ offset) for i in range(dev_size)])

    loaded = []
    taken = 0
    for k, (low, members) in enumerate(groups):
        got = [swap(held, offset << low) for offset in range(1, members)]
        if k < len(LOADS):
            loaded.append(load(k, taken))
            taken += LOADS[k] * tk
        held = pl.pallas_call(
            functools.partial(merge_kernel, low=low),
            out_shape=jax.ShapeDtypeStruct((members * held.shape[0], packed_width), jnp.bfloat16),
            in_specs=[SM] + [VM] * members,
            out_specs=VM,
            compiler_params=pltpu.CompilerParams(vmem_limit_bytes=6 << 20),
        )(me_arr, held, *got)
    other = role_swap(held)

    low, members = groups[-1]
    parts = role_size * members
    size = half // members
    own, *rest = pl.pallas_call(
        functools.partial(
            expert_kernel, tk=tk, tn=tn, base=width + LANES, rows=rows, slices=slices,
            groups=groups, loads=len(loaded), parts=parts,
        ),
        out_shape=[jax.ShapeDtypeStruct((size, width), jnp.float32)]
        + [jax.ShapeDtypeStruct((size, width), jnp.bfloat16)] * (parts - 1)
        + [jax.ShapeDtypeStruct((dev_size,) + swap_pool.shape[1:], jnp.bfloat16)] * 2,
        in_specs=[SM, VM, VM] + [VM] * len(loaded) + [HBM] * 4,
        out_specs=[VM] * (parts + 2),
        scratch_shapes=[
            pltpu.VMEM((GATE_SLOTS, tk, units), jnp.bfloat16),
            pltpu.VMEM((UP_SLOTS, tk, units), jnp.bfloat16),
            pltpu.VMEM((DOWN_SLOTS, units, tn), jnp.bfloat16),
            pltpu.VMEM((total_rows, units), jnp.float32),
            pltpu.VMEM((total_rows, units), jnp.float32),
            pltpu.VMEM((total_rows, units), jnp.bfloat16),
            pltpu.VMEM((total_rows, 1), jnp.float32),
            pltpu.VMEM((total_rows, id_cols), jnp.int32),
            pltpu.SMEM((total_rows, id_cols), jnp.int32),
            pltpu.SemaphoreType.DMA((GATE_SLOTS,)),
            pltpu.SemaphoreType.DMA((UP_SLOTS,)),
            pltpu.SemaphoreType.DMA((DOWN_SLOTS,)),
            pltpu.SemaphoreType.DMA,
            pltpu.SemaphoreType.DMA((2,)),
        ],
        compiler_params=pltpu.CompilerParams(vmem_limit_bytes=36 << 20),
        cost_estimate=pl.CostEstimate(
            flops=6 * total_rows * width * units, bytes_accessed=3 * weight_bytes, transcendentals=0
        ),
    )(me_arr, held, other, *loaded, *weights_in, pool_in)

    sends, near, far = rest[:-2], rest[-2], rest[-1]
    far = role_swap(far)
    got = []
    for n, value in enumerate(sends):
        flat = ((n + 1) // members) * dev_size + (((n + 1) % members) << low)
        got.append(lax.ppermute(value, ("role", "dev"), [(i, i ^ flat) for i in range(devices)]))
    page_shape = (dev_size, swap_pool.shape[1], 2 * swap_pool.shape[2])
    outgoing = pl.pallas_call(
        stack_kernel,
        out_shape=jax.ShapeDtypeStruct(page_shape, jnp.bfloat16),
        in_specs=[VM, VM],
        out_specs=HBM,
        scratch_shapes=[
            pltpu.VMEM((dev_size, swap_pool.shape[1], 2 * ROPE), jnp.bfloat16),
            pltpu.SemaphoreType.DMA((3,)),
        ],
        compiler_params=pltpu.CompilerParams(vmem_limit_bytes=8 << 20),
    )(near, far)
    arrived = lax.all_to_all(outgoing, "dev", split_axis=0, concat_axis=0, tiled=True)
    for low, members in reversed(groups[:-1]):
        count = own.shape[0] // members
        own, *sends = pl.pallas_call(
            functools.partial(fold_kernel, low=low, members=members, arrived=len(got)),
            out_shape=[jax.ShapeDtypeStruct((count, width), jnp.float32)]
            + [jax.ShapeDtypeStruct((count, width), jnp.bfloat16)] * (members - 1),
            in_specs=[SM] + [VM] * (1 + len(got)),
            out_specs=[VM] * members,
            compiler_params=pltpu.CompilerParams(vmem_limit_bytes=16 << 20),
        )(me_arr, own, *got)
        got = [swap(value, (n + 1) << low) for n, value in enumerate(sends)]
    query_rows = queries.shape[0] * queries.shape[1]
    bias, peaks, sums, local_out = pl.pallas_call(
        early_kernel,
        out_shape=(
            jax.ShapeDtypeStruct((query_rows, devices * swap_pool.shape[1]), jnp.float32),
            jax.ShapeDtypeStruct((query_rows, 1), jnp.float32),
            jax.ShapeDtypeStruct((query_rows, 1), jnp.float32),
            jax.ShapeDtypeStruct((query_rows, queries.shape[2] - ROPE), jnp.float32),
        ),
        in_specs=[SM] * 2 + [VM] * 3,
        out_specs=(VM,) * 4,
        compiler_params=pltpu.CompilerParams(vmem_limit_bytes=16 << 20),
    )(me_arr, cache_lengths, page_owner, queries, local_cache)
    operands = (bias, peaks, sums, local_out, queries, arrived, hidden, own, *got)
    attn_out, moe_out = pl.pallas_call(
        finish_kernel,
        out_shape=(
            jax.ShapeDtypeStruct(queries.shape[:2] + (queries.shape[2] - ROPE,), jnp.bfloat16),
            jax.ShapeDtypeStruct(hidden.shape, jnp.bfloat16),
        ),
        in_specs=[VM] * len(operands),
        out_specs=(VM, VM),
        compiler_params=pltpu.CompilerParams(vmem_limit_bytes=24 << 20),
    )(*operands)
    return (attn_out, moe_out)


def solution(mesh):
    in_specs = (
        P(("group", "role", "dev"), None),
        P(),
        P(("group", "role", "dev"), None),
        P(("group", "role", "dev"), None),
        P(None, ("role", "dev")),
        P(None, ("role", "dev")),
        P(("role", "dev"), None),
        P(("group", "role", "dev"), None, None),
        P(("group", "role", "dev"), None, None),
        P(("group", "role", "dev")),
        P(("group", "role", "dev"), None, None),
        P(("group", "role", "dev"), None),
        P(("group", "role", "dev"), None),
    )
    out_specs = (P(("group", "role", "dev"), None, None), P(("group", "role", "dev"), None))
    return jax.shard_map(per_device, mesh=mesh, in_specs=in_specs, out_specs=out_specs, check_vma=False)
```
